256 devices in a mesh: ctx: 128 (over z, x_lo, y, core), ch: 2 (over x_hi).
Axes of the slice: x: 4 (x_hi: 2, x_lo: 2; x = x_hi * 2 + x_lo), y: 4, z: 8, core: 2. Of those that a mesh axis runs over, the one named last changes fastest.
Arguments:
- query_proj: bfloat16 [32768, 2048], P('ctx', 'ch'), may hold values from -64 to 64
- key_proj: bfloat16 [32768, 2048], P('ctx', 'ch'), may hold values from -6 to 6
- value_proj: bfloat16 [32768, 2048], P('ctx', 'ch'), may hold values from -6 to 6
- filters: bfloat16 [1024, 2048], P('ctx', 'ch'), may hold values from -0.1875 to 0.1875
- cotangent: bfloat16 [32768, 2048], P('ctx', 'ch'), may hold values from -6 to 6
- stock_id: int32 [32768], P('ctx'), may hold values from 0 to 511
- stock_class: int32 [512], replicated, may hold values from 0 to 10
- cond_table: float32 [11, 2048], P(None, 'ch'), may hold values from -2.5 to 2.5
Outputs:
- normed_out: bfloat16 [32768, 2048], P('ctx', 'ch')
- grad_query: bfloat16 [32768, 2048], P('ctx', 'ch')
- grad_key: bfloat16 [32768, 2048], P('ctx', 'ch')
- grad_value: bfloat16 [32768, 2048], P('ctx', 'ch')
- grad_filter: float32 [1024, 2048], P('ctx', 'ch')
The draws below stay inside these ranges and needn't reach their ends.
All inputs are finite; a program needn't handle non-finite values.
Results may differ from the reference program's by a relative error of at most 0.005.
Values may be sent and summed in bfloat16 or wider, within the bound.
No kernel may reach another device: no remote copies, remote signals or barrier semaphores. Data moves between devices by JAX's collectives and lax.ppermute only.
A program may use at most 128 MiB of HBM per device.

```python
import functools
import math
import jax
import jax.numpy as jnp
import numpy as np
from jax import lax

CH = 2048
NSTOCK = 512
NCLASS = 11
TOKENS = 32768
FILT = 1024


def draw_query_proj(key, part):
    first_key, second_key = jax.random.split(key)
    column = jnp.arange(CH, dtype=jnp.float32) / (CH - 1)
    column_scale = jnp.exp((column - 0.5) * 2.302585)
    base = jnp.clip(jax.random.normal(first_key, (TOKENS, CH), jnp.float32), -6.0, 6.0)
    row_scale = jnp.exp(jax.random.uniform(second_key, (TOKENS, 1), jnp.float32, -1.1513, 1.1513))
    return (base * row_scale * column_scale[None, :]).astype(jnp.bfloat16)


def set_ends(drawn, rng, least, largest):
    spot = [jax.random.randint(jax.random.fold_in(rng, axis), (), 0, length) for axis, length in enumerate(drawn.shape)]
    longest = drawn.shape.index(max(drawn.shape))
    neighbour = spot[:longest] + [(spot[longest] + 1) % drawn.shape[longest]] + spot[longest + 1:]
    return drawn.at[tuple(spot)].set(least).at[tuple(neighbour)].set(largest)


def block_levels(rng, shape, pieces, smallest, largest):
    loudness, own = 1.0, jax.random.fold_in(rng, 6)
    for dim, parts in pieces:
        heights = jnp.exp(jax.random.uniform(jax.random.fold_in(own, dim), (parts,), jnp.float32, smallest / len(pieces), largest / len(pieces)))
        loudness = loudness * jnp.repeat(heights, shape[dim] // parts).reshape([-1 if axis == dim else 1 for axis in range(len(shape))])
    return loudness


def rank_bounds(number_of, slope):
    portions = [(1 << 20) // math.isqrt(grade ** slope) + 1 for grade in range(1, number_of + 1)]
    spread = 1 + sum(portions) // (1 << 30)
    return np.cumsum(np.array([max(1, weight // spread) for weight in portions]))


def skewed_ids(stream_key, dims, count, slope):
    table = rank_bounds(count, slope)
    pick = jax.random.randint(jax.random.fold_in(stream_key, 1), dims, 0, int(table[count - 1]))
    standing = jnp.searchsorted(jnp.asarray(table, jnp.int32), pick, side="right")
    return jax.random.permutation(jax.random.fold_in(stream_key, 2), count)[standing].astype(jnp.int32)


def normal_values(rng, shape, scale, most, cuts=(), held_as=jnp.bfloat16):
    entries = jax.random.normal(rng, shape, jnp.float32) * scale
    if len(cuts) > 0:
        entries = block_levels(rng, shape, cuts, -0.22, 0.18) * entries
    return jnp.clip(entries, min=-most, max=most).astype(held_as)


def setup_inputs(seed: int = 0) -> dict:
    arg_keys = jax.random.split(jax.random.key(seed), 9)
    query_proj = draw_query_proj(jax.random.fold_in(arg_keys[8], 71), 0)
    key_proj = normal_values(arg_keys[1], (TOKENS, CH), 1.0, 6.0, ((0, 128), (1, 2)))
    value_proj = normal_values(arg_keys[2], (TOKENS, CH), 1.0, 6.0, ((0, 128), (1, 2)))
    filters = normal_values(arg_keys[3], (FILT, CH), FILT ** -0.5, 0.1875, ((0, 128), (1, 2)))
    cotangent = normal_values(arg_keys[4], (TOKENS, CH), 1.0, 6.0, ((0, 128), (1, 2)))
    stock_id = set_ends(skewed_ids(arg_keys[5], (TOKENS,), NSTOCK, 2), jax.random.fold_in(arg_keys[5], 3), 0, NSTOCK - 1).astype(jnp.int32)
    stock_class = set_ends(jax.random.randint(arg_keys[6], (NSTOCK,), 0, NCLASS), jax.random.fold_in(arg_keys[6], 1), 0, NCLASS - 1).astype(jnp.int32)
    cond_table = normal_values(arg_keys[7], (NCLASS, CH), 0.5, 2.5, ((1, 2),), jnp.float32)
    return {"query_proj": query_proj, "key_proj": key_proj, "value_proj": value_proj, "filters": filters, "cotangent": cotangent, "stock_id": stock_id, "stock_class": stock_class, "cond_table": cond_table}


EPSILON = 1e-05

def fft_length(first_len, second_len):
    return 1 << (first_len + second_len - 1).bit_length()

def grouped(function, arrays):
    channels = arrays[0].shape[1]
    group_width = math.gcd(channels, 128)
    stacked = tuple((array_in.reshape(array_in.shape[0], channels // group_width, group_width).transpose(1, 0, 2) for array_in in arrays))
    result = lax.map(lambda members: function(*members), stacked)
    return result.transpose(1, 0, 2).reshape(result.shape[1], channels)

def causal_conv(signal_in, kernel):
    length_fft = fft_length(signal_in.shape[0], kernel.shape[0])
    spectrum = jnp.fft.rfft(signal_in, n=length_fft, axis=0) * jnp.fft.rfft(kernel, n=length_fft, axis=0)
    return jnp.fft.irfft(spectrum, n=length_fft, axis=0)[:signal_in.shape[0]]

def anti_causal(signal_in, kernel):
    return causal_conv(signal_in[::-1], kernel)[::-1]

def correlate(later_rows, earlier, lag_count):
    length_fft = fft_length(later_rows.shape[0], lag_count)
    spectrum = jnp.fft.rfft(later_rows, n=length_fft, axis=0) * jnp.conj(jnp.fft.rfft(earlier, n=length_fft, axis=0))
    return jnp.fft.irfft(spectrum, n=length_fft, axis=0)[:lag_count]

def reference(query_proj, key_proj, value_proj, filters, cotangent, stock_id, stock_class, cond_table):
    event_class = jnp.take(stock_class, stock_id, axis=0).astype(jnp.int32)
    cond_rows = jnp.take(cond_table, event_class, axis=0).astype(jnp.float32)
    gate_rows = query_proj.astype(jnp.float32) * (1.0 + cond_rows)
    mixed_in = (key_proj.astype(jnp.float32) * value_proj.astype(jnp.float32)).astype(jnp.bfloat16)
    mixed_wide = mixed_in.astype(jnp.float32)
    filter_wide = filters.astype(jnp.float32)
    conv_out = grouped(causal_conv, (mixed_wide, filter_wide))
    scaled = gate_rows * conv_out
    inv_rms = lax.rsqrt(lax.optimization_barrier(jnp.mean(scaled * scaled, axis=1, keepdims=True)) + EPSILON)
    normed = scaled * inv_rms
    normed_out = normed.astype(jnp.bfloat16)
    upstream = cotangent.astype(jnp.float32)
    inner_mean = lax.optimization_barrier(jnp.mean(upstream * normed, axis=1, keepdims=True))
    grad_scaled = inv_rms * (upstream - normed * inner_mean)
    grad_query = (grad_scaled * conv_out * (1.0 + cond_rows)).astype(jnp.bfloat16)
    grad_conv = (grad_scaled * gate_rows).astype(jnp.bfloat16)
    grad_wide = grad_conv.astype(jnp.float32)
    grad_mixed = grouped(anti_causal, (grad_wide, filter_wide))
    grad_key = (grad_mixed * value_proj.astype(jnp.float32)).astype(jnp.bfloat16)
    grad_value = (grad_mixed * key_proj.astype(jnp.float32)).astype(jnp.bfloat16)
    grad_filter = grouped(functools.partial(correlate, lag_count=filters.shape[0]), (grad_wide, mixed_wide))
    return (normed_out, grad_query, grad_key, grad_value, grad_filter.astype(jnp.float32))
```

```python
import functools

import jax
import jax.numpy as jnp
import numpy as np
import ml_dtypes
from jax import lax
from jax.experimental import pallas as pl
from jax.experimental.pallas import tpu as pltpu
from jax.sharding import Mesh, PartitionSpec as P

GROUP = 8
REACH = 4
LEN = 256
LANES = 128
EPSILON = 1e-05
F32 = jnp.float32
BF16 = jnp.bfloat16


def split_table(table):
    high = table.astype(np.float32).astype(ml_dtypes.bfloat16)
    low = (table - high.astype(np.float64)).astype(ml_dtypes.bfloat16)
    return high, low


def transform_tables():
    number = np.concatenate([np.arange(0, LEN, 2), np.arange(1, LEN, 2)])
    angles = np.pi * ((2 * number[:, None] + 1) * np.arange(LEN)[None, :] % (4 * LEN)) / (2 * LEN)
    forward = np.concatenate([np.cos(angles), -np.sin(angles)], axis=0)
    return (*split_table(forward), *split_table(forward.T / LEN))


def dot(left, right):
    return jnp.dot(left, right, preferred_element_type=F32)


def halves(value):
    high = value.astype(BF16)
    return high, (value - high.astype(F32)).astype(BF16)


def lane(index):
    return pl.ds(pl.multiple_of(index * LANES, LANES), LANES)


def col(index):
    return slice(index * LANES, (index + 1) * LANES)


def pack_mixed(key_ref, value_ref, filters_ref, out_ref):
    for place in range(GROUP):
        product = key_ref[:, col(place)].astype(F32) * value_ref[:, col(place)].astype(F32)
        out_ref[place, :LEN, :] = product.astype(BF16)
        out_ref[place, LEN:, :] = filters_ref[:, col(place)]


def pack_gates(place_ref, query_ref, cotangent_ref, stock_ref, class_ref, *out_refs):
    place = place_ref[0]
    stocks = class_ref.shape[1]
    hits = (lax.broadcasted_iota(jnp.int32, (stocks, LEN), 0) == stock_ref[...]).astype(F32).astype(BF16)
    classes = jnp.broadcast_to(class_ref[...].astype(F32), (8, stocks)).astype(BF16)
    event_class = dot(classes, hits).astype(BF16)
    for step in range(GROUP):
        there = lane((place + step) & (GROUP - 1))
        out_refs[step][:LEN, :] = query_ref[:, there]
        out_refs[step][LEN : 2 * LEN, :] = cotangent_ref[:, there]
        out_refs[step][2 * LEN : 2 * LEN + 8, :] = event_class[:, :LANES]
        out_refs[step][2 * LEN + 8 :, :] = event_class[:, LANES:]


def unpack_gates(place_ref, table_ref, *refs):
    pieces, (gate_ref, factor_ref, upstream_ref) = refs[:GROUP], refs[GROUP:]
    place = place_ref[0]
    table = table_ref[:, lane(place)]
    table_high, rest = table.astype(BF16), table
    table_mid = (rest - table_high.astype(F32)).astype(BF16)
    table_low = (rest - table_high.astype(F32) - table_mid.astype(F32)).astype(BF16)
    rows = table.shape[0]
    for step in range(GROUP):
        there = lane((place - step) & (GROUP - 1))
        piece = pieces[step]
        event_class = jnp.concatenate(
            [piece[2 * LEN : 2 * LEN + 8, :].astype(F32)[:1], piece[2 * LEN + 8 :, :].astype(F32)[:1]], axis=1
        )
        number = lax.broadcasted_iota(jnp.int32, (rows, LEN), 0).astype(F32)
        hits = (number == event_class).astype(F32)
        hits = jnp.transpose(hits).astype(BF16)
        factor = 1.0 + (dot(hits, table_high) + dot(hits, table_mid) + dot(hits, table_low))
        factor_ref[:, there] = factor
        gate_ref[:, there] = piece[:LEN, :].astype(F32) * factor
        upstream_ref[:, there] = piece[LEN : 2 * LEN, :]


def spectrum(forward, rows):
    return dot(forward[0][...], rows) + dot(forward[1][...], rows)


def invert(inverse, spec):
    high, low = halves(spec)
    return dot(inverse[0][...], high) + (dot(inverse[0][...], low) + dot(inverse[1][...], high))


def over_frequencies(step):
    for half in range(2):
        @pl.loop(0, LEN // 16)
        def _(chunk):
            step(pl.multiple_of(half * (LEN // 2) + chunk * 8, 8), 1.0 - 2.0 * half)


def own_spectra(mixed_ref, forward_high, forward_low, out_ref):
    rows = jnp.concatenate([mixed_ref[block, :LEN, :] for block in range(GROUP)], axis=1)
    out_ref[...] = spectrum((forward_high, forward_low), rows)


def windows(real, imag, sign):
    pairs = {}
    for block in range(1, len(real)):
        pairs[block] = (real[block] - sign * imag[block - 1], imag[block] + sign * real[block - 1])
    return pairs


def read_blocks(own_ref, before_ref, row):
    real = [before_ref[pl.ds(row, 8), col(block)] for block in range(REACH)]
    real += [own_ref[pl.ds(row, 8), col(block)] for block in range(GROUP)]
    imag = [before_ref[pl.ds(row + LEN, 8), col(block)] for block in range(REACH)]
    imag += [own_ref[pl.ds(row + LEN, 8), col(block)] for block in range(GROUP)]
    return real, imag


def convolve(
    own_ref, before_ref, lags_ref, gate_ref, upstream_ref, forward_high, forward_low, inverse_high, inverse_low,
    conv_ref, before_spec_ref, lag_spec_ref, sums_ref, product_ref,
):
    forward = (forward_high, forward_low)
    before_spec_ref[...] = spectrum(forward, jnp.concatenate([before_ref[b] for b in range(REACH)], axis=1))
    lags = lags_ref[...].reshape(REACH, LEN, LANES)
    lag_spec_ref[...] = spectrum(forward, jnp.concatenate([lags[b] for b in range(REACH)], axis=1))

    def step(row, sign):
        real, imag = read_blocks(own_ref, before_spec_ref, row)
        pairs = windows(real, imag, sign)
        lag = [
            (lag_spec_ref[pl.ds(row, 8), col(d)], lag_spec_ref[pl.ds(row + LEN, 8), col(d)]) for d in range(REACH)
        ]
        for block in range(GROUP):
            total_real, total_imag = 0.0, 0.0
            for d in range(REACH):
                window = pairs[REACH + block - d]
                total_real += lag[d][0] * window[0] - lag[d][1] * window[1]
                total_imag += lag[d][0] * window[1] + lag[d][1] * window[0]
            product_ref[pl.ds(row, 8), col(block)] = total_real
            product_ref[pl.ds(row + LEN, 8), col(block)] = total_imag

    over_frequencies(step)
    conv = invert((inverse_high, inverse_low), product_ref[...])
    conv_ref[...] = conv
    scaled = gate_ref[...] * conv
    ones = jnp.ones((8, LANES), BF16)
    upstream = upstream_ref[...].astype(F32)

    def channel_sum(value):
        parts = halves(value)
        contract = (((1,), (1,)), ((), ()))
        return sum(lax.dot_general(ones, part, contract, preferred_element_type=F32) for part in parts)

    for index, value in enumerate((scaled * scaled, scaled * upstream)):
        for pair in range(GROUP // 2):
            both = jnp.concatenate(
                [channel_sum(value[:, col(2 * pair)])[:1], channel_sum(value[:, col(2 * pair + 1)])[:1]], axis=1
            )
            line = index * (GROUP // 2) + pair
            for peer in range(sums_ref.shape[0]):
                sums_ref[peer, line : line + 1, :] = both


def finish_norm(
    channels, place_ref, sums_ref, conv_ref, gate_ref, factor_ref, upstream_ref, grad_ref, first_ref, *refs
):
    out_refs, both_ref = refs[:GROUP], refs[GROUP]
    place = place_ref[0]
    total = jnp.sum(sums_ref[...], axis=0)
    half = GROUP // 2
    inv_rms = lax.rsqrt(total[:half] / channels + EPSILON)
    inner = total[half:] * inv_rms / channels
    lines = jnp.transpose(jnp.concatenate([inv_rms, inner], axis=0))
    for block in range(GROUP):
        rows = slice((block % 2) * LEN, (block % 2 + 1) * LEN)
        inv = lines[rows, block // 2 : block // 2 + 1]
        mean = lines[rows, half + block // 2 : half + block // 2 + 1]
        conv, gate = conv_ref[:, col(block)], gate_ref[:, col(block)]
        normed = gate * conv * inv
        both_ref[:LEN, col(block)] = normed.astype(BF16)
        grad_scaled = inv * (upstream_ref[:, col(block)].astype(F32) - normed * mean)
        both_ref[LEN:, col(block)] = (grad_scaled * conv * factor_ref[:, col(block)]).astype(BF16)
        grad_conv = (grad_scaled * gate).astype(BF16)
        grad_ref[:, col(block)] = grad_conv
        if block < REACH:
            first_ref[:, col(block)] = grad_conv
    for step in range(GROUP):
        out_refs[step][...] = both_ref[:, lane((place + step) & (GROUP - 1))]


def filter_terms(
    grad_ref, own_ref, before_ref, forward_high, forward_low, inverse_high, inverse_low, grad_spec_ref, out_ref,
    product_ref,
):
    grad_spec_ref[...] = spectrum((forward_high, forward_low), grad_ref[...])

    def step(row, sign):
        real, imag = read_blocks(own_ref, before_ref, row)
        pairs = windows(real, imag, sign)
        grads = [
            (grad_spec_ref[pl.ds(row, 8), col(b)], grad_spec_ref[pl.ds(row + LEN, 8), col(b)]) for b in range(GROUP)
        ]
        for d in range(REACH):
            total_real, total_imag = 0.0, 0.0
            for block in range(GROUP):
                window = pairs[REACH + block - d]
                total_real += grads[block][0] * window[0] + grads[block][1] * window[1]
                total_imag += grads[block][1] * window[0] - grads[block][0] * window[1]
            product_ref[pl.ds(row, 8), col(d)] = total_real
            product_ref[pl.ds(row + LEN, 8), col(d)] = total_imag

    over_frequencies(step)
    terms = invert((inverse_high, inverse_low), product_ref[...])
    owners, rows = out_ref.shape[0] // REACH, out_ref.shape[1]
    for d in range(REACH):
        out_ref[d * owners : (d + 1) * owners] = terms[:, col(d)].reshape(owners, rows, LANES)


def correlate_back(
    place_ref, grad_spec_ref, after_ref, lag_spec_ref, forward_high, forward_low, inverse_high, inverse_low, *refs
):
    out_refs, (after_spec_ref, product_ref, result_ref) = refs[:GROUP], refs[GROUP:]
    place = place_ref[0]
    after_spec_ref[...] = spectrum((forward_high, forward_low), after_ref[...])

    def step(row, sign):
        real = [grad_spec_ref[pl.ds(row, 8), col(b)] for b in range(GROUP)]
        real += [after_spec_ref[pl.ds(row, 8), col(b)] for b in range(REACH)]
        imag = [grad_spec_ref[pl.ds(row + LEN, 8), col(b)] for b in range(GROUP)]
        imag += [after_spec_ref[pl.ds(row + LEN, 8), col(b)] for b in range(REACH)]
        pairs = [
            (real[b] + sign * imag[b + 1], imag[b] - sign * real[b + 1]) for b in range(GROUP + REACH - 1)
        ]
        lag = [
            (lag_spec_ref[pl.ds(row, 8), col(d)], lag_spec_ref[pl.ds(row + LEN, 8), col(d)]) for d in range(REACH)
        ]
        for block in range(GROUP):
            total_real, total_imag = 0.0, 0.0
            for d in range(REACH):
                window = pairs[block + d]
                total_real += lag[d][0] * window[0] + lag[d][1] * window[1]
                total_imag += lag[d][0] * window[1] - lag[d][1] * window[0]
            product_ref[pl.ds(row, 8), col(block)] = total_real
            product_ref[pl.ds(row + LEN, 8), col(block)] = total_imag

    over_frequencies(step)
    result_ref[...] = invert((inverse_high, inverse_low), product_ref[...]).astype(BF16)
    for step_number in range(GROUP):
        out_refs[step_number][...] = result_ref[:, lane((place + step_number) & (GROUP - 1))]


def finish_forward(place_ref, *refs):
    pieces, (normed_ref, grad_query_ref) = refs[:GROUP], refs[GROUP:]
    place = place_ref[0]
    for step in range(GROUP):
        there = lane((place - step) & (GROUP - 1))
        normed_ref[:, there] = pieces[step][:LEN, :]
        grad_query_ref[:, there] = pieces[step][LEN:, :]


def finish_backward(place_ref, key_ref, value_ref, *refs):
    pieces, (grad_key_ref, grad_value_ref) = refs[:GROUP], refs[GROUP:]
    place = place_ref[0]
    for step in range(GROUP):
        there = lane((place - step) & (GROUP - 1))
        grad_mixed = pieces[step][...].astype(F32)
        grad_key_ref[:, there] = (grad_mixed * value_ref[:, there].astype(F32)).astype(BF16)
        grad_value_ref[:, there] = (grad_mixed * key_ref[:, there].astype(F32)).astype(BF16)


def sum_terms(terms_ref, out_ref):
    groups = terms_ref.shape[0] // GROUP
    for place in range(GROUP):
        total = terms_ref[place]
        for group in range(1, groups):
            total = total + terms_ref[group * GROUP + place]
        out_ref[:, col(place)] = total


def call(body, outs, *args, scalars=0, scratch=(), cost=None):
    specs = [pl.BlockSpec(memory_space=pltpu.SMEM)] * scalars
    specs += [pl.BlockSpec(memory_space=pltpu.VMEM)] * (len(args) - scalars)
    shapes = [jax.ShapeDtypeStruct(shape, dtype) for shape, dtype in outs]
    moved = sum(a.size * a.dtype.itemsize for a in args) + sum(s.size * s.dtype.itemsize for s in shapes)
    return pl.pallas_call(
        body,
        out_shape=shapes,
        in_specs=specs,
        out_specs=[pl.BlockSpec(memory_space=pltpu.VMEM)] * len(shapes),
        scratch_shapes=[pltpu.VMEM(shape, dtype) for shape, dtype in scratch],
        cost_estimate=pl.CostEstimate(flops=cost or 1000, bytes_accessed=moved, transcendentals=0),
    )(*args)


def swap(pieces):
    return [pieces[0]] + [
        lax.ppermute(pieces[step], "j", [(i, (i + step) % GROUP) for i in range(GROUP)]) for step in range(1, GROUP)
    ]


def shards(query_proj, key_proj, value_proj, filters, cotangent, stock_id, stock_class, cond_table):
    groups = lax.axis_size("g")
    parts = lax.axis_size("ch")
    lag_rows = filters.shape[0]
    wide = GROUP * LANES
    place = lax.axis_index("j").astype(jnp.int32)[None]
    forward_high, forward_low, inverse_high, inverse_low = (jnp.asarray(t) for t in transform_tables())
    forward, inverse = (forward_high, forward_low), (inverse_high, inverse_low)

    (sent,) = call(pack_mixed, [((GROUP, LEN + lag_rows, LANES), BF16)], key_proj, value_proj, filters)
    got = lax.all_to_all(sent, "j", 0, 0)
    gates = call(
        pack_gates, [((2 * LEN + 16, LANES), BF16)] * GROUP, place, query_proj, cotangent, stock_id[None, :],
        stock_class[None, :], scalars=1,
    )
    lags = got[:, LEN:, :].reshape(1, GROUP * lag_rows, LANES)
    lags = lax.all_to_all(jnp.broadcast_to(lags, (groups, *lags.shape[1:])), "g", 0, 0)
    before = lax.ppermute(got[GROUP - REACH :, :LEN, :], "g", [(i, i + 1) for i in range(groups - 1)])
    gates = swap(gates)
    (own,) = call(own_spectra, [((2 * LEN, wide), F32)], got, *forward, cost=2 * 4 * LEN * LEN * wide)
    table = jnp.pad(cond_table, ((0, 16 - cond_table.shape[0]), (0, 0)))
    gate, factor, upstream = call(
        unpack_gates, [((LEN, wide), F32), ((LEN, wide), F32), ((LEN, wide), BF16)], place, table, *gates, scalars=1
    )
    conv, before_spec, lag_spec, sums = call(
        convolve,
        [((LEN, wide), F32), ((2 * LEN, wide // 2), F32), ((2 * LEN, wide // 2), F32), ((GROUP * parts, 8, 2 * LEN), F32)],
        own, before, lags.reshape(REACH * LEN, LANES), gate, upstream, *forward, *inverse,
        scratch=[((2 * LEN, wide), F32)], cost=2 * 10 * LEN * LEN * wide,
    )
    sums = lax.all_to_all(sums, ("j", "ch"), 0, 0)
    results = call(
        functools.partial(finish_norm, wide * parts),
        [((LEN, wide), BF16), ((LEN, wide // 2), BF16)] + [((2 * LEN, LANES), BF16)] * GROUP,
        place, sums, conv, gate, factor, upstream, scalars=1, scratch=[((2 * LEN, wide), BF16)],
    )
    grad_conv, first, both = results[0], results[1], results[2:]
    after = lax.ppermute(first, "g", [(i, i - 1) for i in range(1, groups)])
    grad_spec, terms = call(
        filter_terms, [((2 * LEN, wide), F32), ((groups * GROUP, lag_rows, LANES), F32)], grad_conv, own, before_spec,
        *forward, *inverse, scratch=[((2 * LEN, wide // 2), F32)], cost=2 * 7 * LEN * LEN * wide,
    )
    terms = lax.all_to_all(terms, ("g", "j"), 0, 0)
    both = swap(both)
    mixed = call(
        correlate_back, [((LEN, LANES), BF16)] * GROUP, place, grad_spec, after, lag_spec, *forward, *inverse, scalars=1,
        scratch=[((2 * LEN, wide // 2), F32), ((2 * LEN, wide), F32), ((LEN, wide), BF16)],
        cost=2 * 8 * LEN * LEN * wide,
    )
    mixed = swap(mixed)
    normed_out, grad_query = call(finish_forward, [((LEN, wide), BF16)] * 2, place, *both, scalars=1)
    grad_key, grad_value = call(
        finish_backward, [((LEN, wide), BF16)] * 2, place, key_proj, value_proj, *mixed, scalars=1
    )
    (grad_filter,) = call(sum_terms, [((lag_rows, wide), F32)], terms)
    return normed_out, grad_query, grad_key, grad_value, grad_filter


def solution(mesh):
    ctx, ch = mesh.devices.shape
    inner = Mesh(mesh.devices.reshape(ctx // GROUP, GROUP, ch), ("g", "j", "ch"))
    rows = ("g", "j")
    return jax.shard_map(
        shards,
        mesh=inner,
        in_specs=(P(rows, "ch"),) * 5 + (P(rows), P(), P(None, "ch")),
        out_specs=(P(rows, "ch"),) * 5,
        check_vma=False,
    )
```

```python
import functools

import jax
import jax.numpy as jnp
import numpy as np
import ml_dtypes
from jax import lax
from jax.experimental import pallas as pl
from jax.experimental.pallas import tpu as pltpu
from jax.sharding import Mesh, PartitionSpec as P

GROUP = 8
REACH = 4
LEN = 256
LANES = 128
EPSILON = 1e-05
F32 = jnp.float32
BF16 = jnp.bfloat16


def split_table(table):
    high = table.astype(np.float32).astype(ml_dtypes.bfloat16)
    low = (table - high.astype(np.float64)).astype(ml_dtypes.bfloat16)
    return high, low


def transform_tables():
    number = np.concatenate([np.arange(0, LEN, 2), np.arange(1, LEN, 2)])
    angles = np.pi * ((2 * number[:, None] + 1) * np.arange(LEN)[None, :] % (4 * LEN)) / (2 * LEN)
    forward = np.concatenate([np.cos(angles), -np.sin(angles)], axis=0)
    return (*split_table(forward), *split_table(forward.T / LEN))


def dot(left, right):
    return jnp.dot(left, right, preferred_element_type=F32)


def halves(value):
    high = value.astype(BF16)
    return high, (value - high.astype(F32)).astype(BF16)


def lane(index):
    return pl.ds(pl.multiple_of(index * LANES, LANES), LANES)


def col(index):
    return slice(index * LANES, (index + 1) * LANES)


def event_classes(stock_ref, class_ref):
    stocks = class_ref.shape[1]
    hits = (lax.broadcasted_iota(jnp.int32, (stocks, LEN), 0) == stock_ref[...]).astype(F32).astype(BF16)
    classes = jnp.broadcast_to(class_ref[...].astype(F32), (8, stocks)).astype(BF16)
    return dot(classes, hits)


def modulation(event_class, table):
    high = table.astype(BF16)
    mid = (table - high.astype(F32)).astype(BF16)
    low = (table - high.astype(F32) - mid.astype(F32)).astype(BF16)
    number = lax.broadcasted_iota(jnp.int32, (table.shape[0], LEN), 0).astype(F32)
    hits = jnp.transpose((number == event_class).astype(F32)).astype(BF16)
    return 1.0 + (dot(hits, high) + dot(hits, mid) + dot(hits, low))


def copy_out(source, target, sem):
    copy = pltpu.make_async_copy(source, target, sem)
    copy.start()
    return copy


QUERY, UPSTREAM, CLASS, ROWS = LEN, 2 * LEN, 3 * LEN, 3 * LEN + 16


def pack(key_ref, value_ref, query_ref, cotangent_ref, stock_ref, class_ref, out_hbm, out_ref, sems):
    event_class = event_classes(stock_ref, class_ref).astype(BF16)
    copies = []
    for place in range(GROUP):
        product = key_ref[:, col(place)].astype(F32) * value_ref[:, col(place)].astype(F32)
        out_ref[place, :LEN, :] = product.astype(BF16)
        out_ref[place, QUERY:UPSTREAM, :] = query_ref[:, col(place)]
        out_ref[place, UPSTREAM:CLASS, :] = cotangent_ref[:, col(place)]
        out_ref[place, CLASS : CLASS + 8, :] = event_class[:, :LANES]
        out_ref[place, CLASS + 8 :, :] = event_class[:, LANES:]
        copies.append(copy_out(out_ref.at[place], out_hbm.at[place], sems.at[place]))
    for copy in copies:
        copy.wait()


def pack_lags(*refs):
    out_ref, first = refs[-1], 0
    for lags_ref in refs[:-1]:
        rows = lags_ref.shape[1]
        for high in range(lags_ref.shape[0]):
            for place in range(GROUP):
                out_ref[place, first : first + rows, :] = lags_ref[high, :, col(place)]
            first += rows


def spectrum(forward, rows):
    return dot(forward[0][...], rows) + dot(forward[1][...], rows)


def invert(inverse, spec):
    high, low = halves(spec)
    return dot(inverse[0][...], high) + (dot(inverse[0][...], low) + dot(inverse[1][...], high))


def over_frequencies(step):
    for half in range(2):
        @pl.loop(0, LEN // 16)
        def _(chunk):
            step(pl.multiple_of(half * (LEN // 2) + chunk * 8, 8), 1.0 - 2.0 * half)


def windows(real, imag, sign):
    pairs = {}
    for block in range(1, len(real)):
        pairs[block] = (real[block] - sign * imag[block - 1], imag[block] + sign * real[block - 1])
    return pairs


def read_blocks(own_ref, before_ref, row):
    real = [before_ref[pl.ds(row, 8), col(block)] for block in range(REACH)]
    real += [own_ref[pl.ds(row, 8), col(block)] for block in range(GROUP)]
    imag = [before_ref[pl.ds(row + LEN, 8), col(block)] for block in range(REACH)]
    imag += [own_ref[pl.ds(row + LEN, 8), col(block)] for block in range(GROUP)]
    return real, imag


def prepare(place_ref, table_ref, got_ref, forward_high, forward_low, own_out, gate_out, own_ref, gate_ref, sems):
    rows = jnp.concatenate([got_ref[b, :LEN, :] for b in range(GROUP)], axis=1)
    own_ref[...] = spectrum((forward_high, forward_low), rows)
    copies = [copy_out(own_ref, own_out, sems.at[0])]
    table = table_ref[:, lane(place_ref[0])]
    for block in range(GROUP):
        classes = got_ref[block, CLASS:, :].astype(F32)
        event_class = jnp.concatenate([classes[:1], classes[8:9]], axis=1)
        gate_ref[:, col(block)] = got_ref[block, QUERY:UPSTREAM, :].astype(F32) * modulation(event_class, table)
    copies.append(copy_out(gate_ref, gate_out, sems.at[1]))
    for copy in copies:
        copy.wait()


def convolve(near_groups, far_groups, place_ref, own_hbm, gate_hbm, got_hbm, before_ref, lags_ref, *refs):
    forward, inverse, outs = refs[:2], refs[2:4], refs[4:9]
    before_spec_ref, lag_spec_ref, conv_ref, rounded_ref, sums_ref = refs[9:14]
    own_ref, gate_ref, upstream_ref, product_ref, sorted_ref, sems = refs[14:]
    loads = [
        copy_out(own_hbm, own_ref, sems.at[0]),
        copy_out(gate_hbm, gate_ref, sems.at[1]),
        copy_out(got_hbm.at[:, UPSTREAM:CLASS, :], upstream_ref, sems.at[2]),
    ]
    group = place_ref[1]
    before_spec_ref[...] = spectrum(forward, jnp.concatenate([before_ref[b] for b in range(REACH)], axis=1))
    rows = lags_ref.shape[1] // (near_groups * far_groups)
    for low in range(near_groups):
        for high in range(far_groups):
            at = (low * far_groups + high) * rows
            first = (group ^ (high * near_groups + low)) * (GROUP * rows)
            row = pl.multiple_of(first & (LEN - 1), GROUP * rows)
            piece = lags_ref[:, at : at + rows, :].astype(F32).reshape(GROUP * rows, LANES)
            sorted_ref[pl.ds(row, GROUP * rows), lane(first // LEN)] = piece
    lag_spec_ref[...] = spectrum(forward, sorted_ref[...].astype(BF16))
    copies = [copy_out(before_spec_ref, outs[0], sems.at[3]), copy_out(lag_spec_ref, outs[1], sems.at[4])]
    loads[0].wait()

    def step(row, sign):
        real, imag = read_blocks(own_ref, before_spec_ref, row)
        pairs = windows(real, imag, sign)
        lag = [
            (lag_spec_ref[pl.ds(row, 8), col(d)], lag_spec_ref[pl.ds(row + LEN, 8), col(d)]) for d in range(REACH)
        ]
        for block in range(GROUP):
            total_real, total_imag = 0.0, 0.0
            for d in range(REACH):
                window = pairs[REACH + block - d]
                total_real += lag[d][0] * window[0] - lag[d][1] * window[1]
                total_imag += lag[d][0] * window[1] + lag[d][1] * window[0]
            product_ref[pl.ds(row, 8), col(block)] = total_real
            product_ref[pl.ds(row + LEN, 8), col(block)] = total_imag

    over_frequencies(step)
    conv = invert(inverse, product_ref[...])
    conv_ref[...] = conv
    rounded_ref[...] = conv.astype(BF16)
    copies += [copy_out(conv_ref, outs[2], sems.at[5]), copy_out(rounded_ref, outs[3], sems.at[6])]
    loads[1].wait()
    loads[2].wait()
    ones = jnp.ones((8, LANES), BF16)

    def channel_sum(value):
        contract = (((1,), (1,)), ((), ()))
        return sum(lax.dot_general(ones, part, contract, preferred_element_type=F32) for part in halves(value))[:1]

    lines = [[], []]
    for block in range(GROUP):
        scaled = gate_ref[:, col(block)] * conv[:, col(block)]
        lines[0].append(channel_sum(scaled * scaled))
        lines[1].append(channel_sum(scaled * upstream_ref[block].astype(F32)))
    for index in range(2):
        for pair in range(GROUP // 2):
            both = jnp.concatenate(lines[index][2 * pair : 2 * pair + 2], axis=1)
            line = index * (GROUP // 2) + pair
            for peer in range(sums_ref.shape[0]):
                sums_ref[peer, line : line + 1, :] = both
    copies.append(copy_out(sums_ref, outs[4], sems.at[7]))
    for copy in copies:
        copy.wait()


def row_lines(channels, sums_ref):
    total = jnp.sum(sums_ref[...], axis=0)
    half = GROUP // 2
    inv_rms = lax.rsqrt(total[:half] / channels + EPSILON)
    return jnp.transpose(jnp.concatenate([inv_rms, total[half:] * inv_rms / channels], axis=0))


def finish_norm(
    channels, sums_ref, conv_hbm, gate_hbm, got_hbm, grad_ref, first_ref, conv_ref, gate_ref, upstream_ref, sems
):
    loads = [
        copy_out(conv_hbm, conv_ref, sems.at[0]),
        copy_out(gate_hbm, gate_ref, sems.at[1]),
        copy_out(got_hbm.at[:, UPSTREAM:CLASS, :], upstream_ref, sems.at[2]),
    ]
    lines = row_lines(channels, sums_ref)
    half = GROUP // 2
    for load in loads:
        load.wait()
    for block in range(GROUP):
        rows = slice((block % 2) * LEN, (block % 2 + 1) * LEN)
        inv = lines[rows, block // 2 : block // 2 + 1]
        mean = lines[rows, half + block // 2 : half + block // 2 + 1]
        gate = gate_ref[:, col(block)]
        normed = gate * conv_ref[:, col(block)] * inv
        grad_conv = (inv * (upstream_ref[block].astype(F32) - normed * mean) * gate).astype(BF16)
        grad_ref[:, col(block)] = grad_conv
        if block < REACH:
            first_ref[:, col(block)] = grad_conv


def filter_terms(
    grad_ref, own_hbm, before_hbm, forward_high, forward_low, inverse_high, inverse_low, spec_out,
    terms_out, product_ref, terms_ref, grad_spec_ref, own_ref, before_ref, sems,
):
    copies = [copy_out(own_hbm, own_ref, sems.at[0]), copy_out(before_hbm, before_ref, sems.at[1])]
    grad_spec_ref[...] = spectrum((forward_high, forward_low), grad_ref[...])
    for copy in copies:
        copy.wait()
    copies = [copy_out(grad_spec_ref, spec_out, sems.at[2])]

    def step(row, sign):
        real, imag = read_blocks(own_ref, before_ref, row)
        pairs = windows(real, imag, sign)
        grads = [
            (grad_spec_ref[pl.ds(row, 8), col(b)], grad_spec_ref[pl.ds(row + LEN, 8), col(b)]) for b in range(GROUP)
        ]
        for d in range(REACH):
            total_real, total_imag = 0.0, 0.0
            for block in range(GROUP):
                window = pairs[REACH + block - d]
                total_real += grads[block][0] * window[0] + grads[block][1] * window[1]
                total_imag += grads[block][1] * window[0] - grads[block][0] * window[1]
            product_ref[pl.ds(row, 8), col(d)] = total_real
            product_ref[pl.ds(row + LEN, 8), col(d)] = total_imag

    over_frequencies(step)
    terms = invert((inverse_high, inverse_low), product_ref[...])
    for d in range(REACH):
        terms_ref[d] = terms[:, col(d)].astype(BF16)
    copies.append(copy_out(terms_ref, terms_out, sems.at[3]))
    for copy in copies:
        copy.wait()


def correlate_back(
    grad_spec_ref, after_ref, lag_spec_ref, forward_high, forward_low, inverse_high, inverse_low, result_ref,
    after_spec_ref, product_ref,
):
    after_spec_ref[...] = spectrum((forward_high, forward_low), after_ref[...])

    def step(row, sign):
        real = [grad_spec_ref[pl.ds(row, 8), col(b)] for b in range(GROUP)]
        real += [after_spec_ref[pl.ds(row, 8), col(b)] for b in range(REACH)]
        imag = [grad_spec_ref[pl.ds(row + LEN, 8), col(b)] for b in range(GROUP)]
        imag += [after_spec_ref[pl.ds(row + LEN, 8), col(b)] for b in range(REACH)]
        pairs = [
            (real[b] + sign * imag[b + 1], imag[b] - sign * real[b + 1]) for b in range(GROUP + REACH - 1)
        ]
        lag = [
            (lag_spec_ref[pl.ds(row, 8), col(d)], lag_spec_ref[pl.ds(row + LEN, 8), col(d)]) for d in range(REACH)
        ]
        for block in range(GROUP):
            total_real, total_imag = 0.0, 0.0
            for d in range(REACH):
                window = pairs[block + d]
                total_real += lag[d][0] * window[0] + lag[d][1] * window[1]
                total_imag += lag[d][0] * window[1] - lag[d][1] * window[0]
            product_ref[pl.ds(row, 8), col(block)] = total_real
            product_ref[pl.ds(row + LEN, 8), col(block)] = total_imag

    over_frequencies(step)
    result_ref[...] = invert((inverse_high, inverse_low), product_ref[...]).astype(BF16)


def pack_back(place_ref, result_ref, rounded_ref, *out_refs):
    for step in range(GROUP):
        there = lane((place_ref[0] + step) & (GROUP - 1))
        out_refs[step][:LEN, :] = result_ref[:, there]
        out_refs[step][LEN:, :] = rounded_ref[:, there]


def sum_terms(terms_ref, out_ref):
    groups = terms_ref.shape[0] // GROUP
    for place in range(GROUP):
        out_ref[:, col(place)] = sum(terms_ref[group * GROUP + place].astype(F32) for group in range(groups))


def finish(
    channels, place_ref, sums_ref, query_ref, key_ref, value_ref, cotangent_ref, stock_ref, class_ref, table_ref, *refs
):
    pieces, (normed_ref, grad_query_ref, grad_key_ref, grad_value_ref, lines_ref) = (
        refs[:GROUP], refs[GROUP:]
    )
    place = place_ref[0]
    half = GROUP // 2
    lines_ref[...] = row_lines(channels, sums_ref)
    lines = lines_ref[pl.ds(pl.multiple_of((place & 1) * LEN, LEN), LEN), :]
    number = lax.broadcasted_iota(jnp.int32, (LEN, GROUP), 1)
    inv = jnp.sum(jnp.where(number == place >> 1, lines, 0.0), axis=1, keepdims=True)
    mean = jnp.sum(jnp.where(number == half + (place >> 1), lines, 0.0), axis=1, keepdims=True)
    event_class = event_classes(stock_ref, class_ref)[:1]
    for step in range(GROUP):
        there = lane((place - step) & (GROUP - 1))
        piece = pieces[step]
        factor = modulation(event_class, table_ref[:, there])
        conv = piece[LEN:, :].astype(F32)
        normed = query_ref[:, there].astype(F32) * factor * conv * inv
        normed_ref[:, there] = normed.astype(BF16)
        grad_scaled = inv * (cotangent_ref[:, there].astype(F32) - normed * mean)
        grad_query_ref[:, there] = (grad_scaled * conv * factor).astype(BF16)
        grad_mixed = piece[:LEN, :].astype(F32)
        grad_key_ref[:, there] = (grad_mixed * value_ref[:, there].astype(F32)).astype(BF16)
        grad_value_ref[:, there] = (grad_mixed * key_ref[:, there].astype(F32)).astype(BF16)


def on_chip(shape, dtype):
    return pltpu.VMEM(shape, dtype)


def off_chip(shape, dtype):
    return pltpu.HBM(shape, dtype)


def near(value):
    return pltpu.with_memory_space_constraint(value, pltpu.VMEM)


def far(value):
    return pltpu.with_memory_space_constraint(value, pltpu.HBM)


def call(body, outs, *args, scalars=0, scratch=(), copies=0, left=(), manual=False, cost=1000):
    specs = [pl.BlockSpec(memory_space=pltpu.SMEM)] * scalars
    specs += [
        pl.BlockSpec(memory_space=pl.ANY if index in left else pltpu.VMEM) for index in range(scalars, len(args))
    ]
    moved = sum(a.size * a.dtype.itemsize for a in args)
    return pl.pallas_call(
        body,
        out_shape=list(outs),
        in_specs=specs,
        out_specs=[pl.BlockSpec(memory_space=pl.ANY if manual else pltpu.VMEM)] * len(outs),
        scratch_shapes=[pltpu.VMEM(shape, dtype) for shape, dtype in scratch]
        + ([pltpu.SemaphoreType.DMA(copies)] if copies else []),
        cost_estimate=pl.CostEstimate(flops=cost, bytes_accessed=moved, transcendentals=0),
        compiler_params=pltpu.CompilerParams(vmem_limit_bytes=20 << 20),
    )(*args)


def swap(pieces):
    return [pieces[0]] + [
        lax.ppermute(pieces[step], "j", [(i, (i + step) % GROUP) for i in range(GROUP)]) for step in range(1, GROUP)
    ]


def trade(value, mask, groups):
    return lax.ppermute(value, "g", [(i, i ^ mask) for i in range(groups)])


def shards(query_proj, key_proj, value_proj, filters, cotangent, stock_id, stock_class, cond_table):
    groups = lax.axis_size("g")
    parts = lax.axis_size("ch")
    near_groups = min(4, groups)
    far_groups = groups // near_groups
    lag_rows = filters.shape[0]
    wide = GROUP * LANES
    half = wide // 2
    place = jnp.stack([lax.axis_index("j"), lax.axis_index("g")]).astype(jnp.int32)
    tables = [jnp.asarray(t) for t in transform_tables()]
    far_tables, near_tables = list(map(far, tables)), list(map(near, tables))
    stock_id, stock_class = far(stock_id[None, :]), far(stock_class[None, :])
    table = far(jnp.pad(cond_table, ((0, 16 - cond_table.shape[0]), (0, 0))))

    (sent,) = call(
        pack, [off_chip((GROUP, ROWS, LANES), BF16)], *map(far, (key_proj, value_proj, query_proj, cotangent)),
        stock_id, stock_class, manual=True, copies=(GROUP,), scratch=[((GROUP, ROWS, LANES), BF16)],
    )
    got = lax.all_to_all(sent, "j", 0, 0)
    lags = filters[None]
    lags = jnp.concatenate([lags] + [trade(lags, high * near_groups, groups) for high in range(1, far_groups)])
    lags = [lags] + [trade(lags, low, groups) for low in range(1, near_groups)]
    (lags,) = call(pack_lags, [off_chip((GROUP, groups * lag_rows, LANES), BF16)], *map(near, lags))
    got, lags = lax.optimization_barrier((got, lags))
    before = lax.ppermute(got[GROUP - REACH :, :LEN, :], "g", [(i, i + 1) for i in range(groups - 1)])
    got, lags = far(got), near(lax.all_to_all(lags, "j", 0, 0))
    own, gate = call(
        prepare, [off_chip((2 * LEN, wide), F32), off_chip((LEN, wide), F32)], place, table, got, *far_tables[:2],
        scalars=1, copies=(2,), manual=True, scratch=[((2 * LEN, wide), F32), ((LEN, wide), F32)],
        cost=2 * 4 * LEN * LEN * wide,
    )
    before_spec, lag_spec, conv, rounded, sums = call(
        functools.partial(convolve, near_groups, far_groups),
        [
            off_chip((2 * LEN, half), F32), off_chip((2 * LEN, half), F32), off_chip((LEN, wide), F32),
            off_chip((LEN, wide), BF16), off_chip((GROUP * parts, 8, 2 * LEN), F32),
        ],
        place, far(own), far(gate), got, before, lags, *far_tables, scalars=1, copies=(8,), manual=True, left=(1, 2, 3),
        scratch=[
            ((2 * LEN, half), F32), ((2 * LEN, half), F32), ((LEN, wide), F32), ((LEN, wide), BF16),
            ((GROUP * parts, 8, 2 * LEN), F32), ((2 * LEN, wide), F32), ((LEN, wide), F32),
            ((GROUP, LEN, LANES), BF16), ((2 * LEN, wide), F32), ((LEN, half), F32),
        ],
        cost=2 * 10 * LEN * LEN * wide,
    )
    sums = lax.all_to_all(sums, ("j", "ch"), 0, 0)
    grad_conv, first = call(
        functools.partial(finish_norm, wide * parts), [on_chip((LEN, wide), BF16), on_chip((LEN, half), BF16)],
        far(sums), far(conv), far(gate), got, left=(1, 2, 3), copies=(3,),
        scratch=[((LEN, wide), F32), ((LEN, wide), F32), ((GROUP, LEN, LANES), BF16)],
    )
    after = lax.ppermute(first, "g", [(i, i - 1) for i in range(1, groups)])
    grad_spec, terms = call(
        filter_terms, [off_chip((2 * LEN, wide), F32), off_chip((REACH, LEN, LANES), BF16)],
        near(grad_conv), far(own), far(before_spec), *far_tables, left=(1, 2), manual=True, copies=(4,),
        scratch=[
            ((2 * LEN, half), F32), ((REACH, LEN, LANES), BF16), ((2 * LEN, wide), F32), ((2 * LEN, wide), F32),
            ((2 * LEN, half), F32),
        ],
        cost=2 * 7 * LEN * LEN * wide,
    )
    terms = lax.all_to_all(terms.reshape(groups * GROUP, lag_rows, LANES), ("g", "j"), 0, 0)
    (back,) = call(
        correlate_back, [off_chip((LEN, wide), BF16)], far(grad_spec), after, far(lag_spec), *far_tables,
        scratch=[((2 * LEN, half), F32), ((2 * LEN, wide), F32)], cost=2 * 8 * LEN * LEN * wide,
    )
    back = call(pack_back, [on_chip((2 * LEN, LANES), BF16)] * GROUP, place, back, rounded, scalars=1)
    back = swap(back)
    (grad_filter,) = call(sum_terms, [off_chip((lag_rows, wide), F32)], terms)
    outs = call(
        functools.partial(finish, wide * parts),
        [off_chip((LEN, wide), BF16)] * 4,
        place, near(sums), *map(near, (query_proj, key_proj, value_proj, cotangent)), stock_id, stock_class, table,
        *map(near, back), scalars=1, scratch=[((2 * LEN, GROUP), F32)],
    )
    return *outs, grad_filter


def solution(mesh):
    ctx, ch = mesh.devices.shape
    inner = Mesh(mesh.devices.reshape(ctx // GROUP, GROUP, ch), ("g", "j", "ch"))
    rows = ("g", "j")
    return jax.shard_map(
        shards,
        mesh=inner,
        in_specs=(P(rows, "ch"),) * 5 + (P(rows), P(), P(None, "ch")),
        out_specs=(P(rows, "ch"),) * 5,
        check_vma=False,
    )
```

```python
import functools

import jax
import jax.numpy as jnp
import numpy as np
import ml_dtypes
from jax import lax
from jax.experimental import pallas as pl
from jax.experimental.pallas import tpu as pltpu
from jax.sharding import Mesh, PartitionSpec as P

GROUP = 8
REACH = 4
LEN = 256
LANES = 128
EPSILON = 1e-05
F32 = jnp.float32
BF16 = jnp.bfloat16


def split_table(table):
    high = table.astype(np.float32).astype(ml_dtypes.bfloat16)
    low = (table - high.astype(np.float64)).astype(ml_dtypes.bfloat16)
    return high, low


def transform_tables():
    number = np.concatenate([np.arange(0, LEN, 2), np.arange(1, LEN, 2)])
    angles = np.pi * ((2 * number[:, None] + 1) * np.arange(LEN)[None, :] % (4 * LEN)) / (2 * LEN)
    forward = np.concatenate([np.cos(angles), -np.sin(angles)], axis=0)
    return (*split_table(forward), *split_table(forward.T / LEN))


def dot(left, right):
    return jnp.dot(left, right, preferred_element_type=F32)


def halves(value):
    high = value.astype(BF16)
    return high, (value - high.astype(F32)).astype(BF16)


def lane(index):
    return pl.ds(pl.multiple_of(index * LANES, LANES), LANES)


def col(index):
    return slice(index * LANES, (index + 1) * LANES)


def event_classes(stock_ref, class_ref):
    stocks = class_ref.shape[1]
    hits = (lax.broadcasted_iota(jnp.int32, (stocks, LEN), 0) == stock_ref[...]).astype(F32).astype(BF16)
    classes = jnp.broadcast_to(class_ref[...].astype(F32), (8, stocks)).astype(BF16)
    return dot(classes, hits)


def modulation(event_class, table):
    high = table.astype(BF16)
    mid = (table - high.astype(F32)).astype(BF16)
    low = (table - high.astype(F32) - mid.astype(F32)).astype(BF16)
    number = lax.broadcasted_iota(jnp.int32, (table.shape[0], LEN), 0).astype(F32)
    hits = jnp.transpose((number == event_class).astype(F32)).astype(BF16)
    return 1.0 + (dot(hits, high) + dot(hits, mid) + dot(hits, low))


def copy_out(source, target, sem):
    copy = pltpu.make_async_copy(source, target, sem)
    copy.start()
    return copy


QUERY, UPSTREAM, CLASS, ROWS = LEN, 2 * LEN, 3 * LEN, 3 * LEN + 16


def pack(key_ref, value_ref, query_ref, cotangent_ref, stock_ref, class_ref, out_hbm, out_ref, sems):
    event_class = event_classes(stock_ref, class_ref).astype(BF16)
    copies = []
    for place in range(GROUP):
        product = key_ref[:, col(place)].astype(F32) * value_ref[:, col(place)].astype(F32)
        out_ref[place, :LEN, :] = product.astype(BF16)
        out_ref[place, QUERY:UPSTREAM, :] = query_ref[:, col(place)]
        out_ref[place, UPSTREAM:CLASS, :] = cotangent_ref[:, col(place)]
        out_ref[place, CLASS : CLASS + 8, :] = event_class[:, :LANES]
        out_ref[place, CLASS + 8 :, :] = event_class[:, LANES:]
        copies.append(copy_out(out_ref.at[place], out_hbm.at[place], sems.at[place]))
    for copy in copies:
        copy.wait()


def pack_lags(*refs):
    out_ref, first = refs[-1], 0
    for lags_ref in refs[:-1]:
        rows = lags_ref.shape[1]
        for high in range(lags_ref.shape[0]):
            for place in range(GROUP):
                out_ref[place, first : first + rows, :] = lags_ref[high, :, col(place)]
            first += rows


def spectrum(forward, rows):
    return dot(forward[0][...], rows) + dot(forward[1][...], rows)


def invert(inverse, spec):
    high, low = halves(spec)
    return dot(inverse[0][...], high) + (dot(inverse[0][...], low) + dot(inverse[1][...], high))


def over_frequencies(step):
    for half in range(2):
        @pl.loop(0, LEN // 16)
        def _(chunk):
            step(pl.multiple_of(half * (LEN // 2) + chunk * 8, 8), 1.0 - 2.0 * half)


def windows(real, imag, sign):
    pairs = {}
    for block in range(1, len(real)):
        pairs[block] = (real[block] - sign * imag[block - 1], imag[block] + sign * real[block - 1])
    return pairs


def read_blocks(own_ref, before_ref, row):
    real = [before_ref[pl.ds(row, 8), col(block)] for block in range(REACH)]
    real += [own_ref[pl.ds(row, 8), col(block)] for block in range(GROUP)]
    imag = [before_ref[pl.ds(row + LEN, 8), col(block)] for block in range(REACH)]
    imag += [own_ref[pl.ds(row + LEN, 8), col(block)] for block in range(GROUP)]
    return real, imag


def prepare(place_ref, table_ref, got_ref, forward_high, forward_low, own_out, gate_out, own_ref, gate_ref, sems):
    rows = jnp.concatenate([got_ref[b, :LEN, :] for b in range(GROUP)], axis=1)
    own_ref[...] = spectrum((forward_high, forward_low), rows)
    copies = [copy_out(own_ref, own_out, sems.at[0])]
    table = table_ref[:, lane(place_ref[0])]
    for block in range(GROUP):
        classes = got_ref[block, CLASS:, :].astype(F32)
        event_class = jnp.concatenate([classes[:1], classes[8:9]], axis=1)
        gate_ref[:, col(block)] = got_ref[block, QUERY:UPSTREAM, :].astype(F32) * modulation(event_class, table)
    copies.append(copy_out(gate_ref, gate_out, sems.at[1]))
    for copy in copies:
        copy.wait()


def convolve(near_groups, far_groups, place_ref, own_hbm, gate_hbm, got_hbm, before_ref, lags_ref, *refs):
    own_ref, gate_ref, upstream_ref, before_spec_ref, conv_ref = refs[4:9]
    forward, inverse = refs[9:11], refs[11:13]
    lag_spec_hbm, rounded_hbm, sums_ref, lag_spec_ref, rounded_ref, product_ref, sorted_ref, sems = refs[13:]
    tables = [copy_out(refs[i], refs[9 + i], sems.at[5 + i]) for i in range(4)]
    loads = [
        copy_out(own_hbm, own_ref, sems.at[0]),
        copy_out(gate_hbm, gate_ref, sems.at[1]),
        copy_out(got_hbm.at[:, UPSTREAM:CLASS, :], upstream_ref, sems.at[2]),
    ]
    group = place_ref[1]
    tables[0].wait()
    tables[1].wait()
    before_spec_ref[...] = spectrum(forward, jnp.concatenate([before_ref[b] for b in range(REACH)], axis=1))
    rows = lags_ref.shape[1] // (near_groups * far_groups)
    for low in range(near_groups):
        for high in range(far_groups):
            at = (low * far_groups + high) * rows
            first = (group ^ (high * near_groups + low)) * (GROUP * rows)
            row = pl.multiple_of(first & (LEN - 1), GROUP * rows)
            piece = lags_ref[:, at : at + rows, :].astype(F32).reshape(GROUP * rows, LANES)
            sorted_ref[pl.ds(row, GROUP * rows), lane(first // LEN)] = piece
    lag_spec_ref[...] = spectrum(forward, sorted_ref[...].astype(BF16))
    copies = [copy_out(lag_spec_ref, lag_spec_hbm, sems.at[4])]
    loads[0].wait()

    def step(row, sign):
        real, imag = read_blocks(own_ref, before_spec_ref, row)
        pairs = windows(real, imag, sign)
        lag = [
            (lag_spec_ref[pl.ds(row, 8), col(d)], lag_spec_ref[pl.ds(row + LEN, 8), col(d)]) for d in range(REACH)
        ]
        for block in range(GROUP):
            total_real, total_imag = 0.0, 0.0
            for d in range(REACH):
                window = pairs[REACH + block - d]
                total_real += lag[d][0] * window[0] - lag[d][1] * window[1]
                total_imag += lag[d][0] * window[1] + lag[d][1] * window[0]
            product_ref[pl.ds(row, 8), col(block)] = total_real
            product_ref[pl.ds(row + LEN, 8), col(block)] = total_imag

    over_frequencies(step)
    tables[2].wait()
    tables[3].wait()
    conv = invert(inverse, product_ref[...])
    conv_ref[...] = conv
    rounded_ref[...] = conv.astype(BF16)
    copies.append(copy_out(rounded_ref, rounded_hbm, sems.at[3]))
    loads[1].wait()
    loads[2].wait()
    ones = jnp.ones((8, LANES), BF16)

    def channel_sum(value):
        contract = (((1,), (1,)), ((), ()))
        return sum(lax.dot_general(ones, part, contract, preferred_element_type=F32) for part in halves(value))[:1]

    lines = [[], []]
    for block in range(GROUP):
        scaled = gate_ref[:, col(block)] * conv[:, col(block)]
        lines[0].append(channel_sum(scaled * scaled))
        lines[1].append(channel_sum(scaled * upstream_ref[block].astype(F32)))
    for index in range(2):
        for pair in range(GROUP // 2):
            both = jnp.concatenate(lines[index][2 * pair : 2 * pair + 2], axis=1)
            line = index * (GROUP // 2) + pair
            for peer in range(sums_ref.shape[0]):
                sums_ref[peer, line : line + 1, :] = both
    for copy in copies:
        copy.wait()


def row_lines(channels, sums_ref):
    total = jnp.sum(sums_ref[...], axis=0)
    half = GROUP // 2
    inv_rms = lax.rsqrt(total[:half] / channels + EPSILON)
    return jnp.transpose(jnp.concatenate([inv_rms, total[half:] * inv_rms / channels], axis=0))


def finish_norm(channels, sums_ref, conv_ref, gate_ref, upstream_ref, grad_ref, first_ref):
    lines = row_lines(channels, sums_ref)
    half = GROUP // 2
    for block in range(GROUP):
        rows = slice((block % 2) * LEN, (block % 2 + 1) * LEN)
        inv = lines[rows, block // 2 : block // 2 + 1]
        mean = lines[rows, half + block // 2 : half + block // 2 + 1]
        gate = gate_ref[:, col(block)]
        normed = gate * conv_ref[:, col(block)] * inv
        grad_conv = (inv * (upstream_ref[block].astype(F32) - normed * mean) * gate).astype(BF16)
        grad_ref[:, col(block)] = grad_conv
        if block < REACH:
            first_ref[:, col(block)] = grad_conv


def filter_terms(
    grad_ref, own_ref, before_ref, forward_high, forward_low, inverse_high, inverse_low, grad_spec_hbm, terms_ref,
    product_ref, grad_spec_ref, sems,
):
    grad_spec_ref[...] = spectrum((forward_high, forward_low), grad_ref[...])
    copy = copy_out(grad_spec_ref, grad_spec_hbm, sems.at[0])

    def step(row, sign):
        real, imag = read_blocks(own_ref, before_ref, row)
        pairs = windows(real, imag, sign)
        grads = [
            (grad_spec_ref[pl.ds(row, 8), col(b)], grad_spec_ref[pl.ds(row + LEN, 8), col(b)]) for b in range(GROUP)
        ]
        for d in range(REACH):
            total_real, total_imag = 0.0, 0.0
            for block in range(GROUP):
                window = pairs[REACH + block - d]
                total_real += grads[block][0] * window[0] + grads[block][1] * window[1]
                total_imag += grads[block][1] * window[0] - grads[block][0] * window[1]
            product_ref[pl.ds(row, 8), col(d)] = total_real
            product_ref[pl.ds(row + LEN, 8), col(d)] = total_imag

    over_frequencies(step)
    terms = invert((inverse_high, inverse_low), product_ref[...])
    for d in range(REACH):
        terms_ref[d] = terms[:, col(d)].astype(BF16)
    copy.wait()


def correlate_back(
    grad_spec_hbm, lag_spec_hbm, after_ref, forward_high, forward_low, inverse_high, inverse_low, result_ref,
    after_spec_ref, product_ref, grad_spec_ref, lag_spec_ref, sems,
):
    loads = [
        copy_out(grad_spec_hbm, grad_spec_ref, sems.at[0]),
        copy_out(lag_spec_hbm, lag_spec_ref, sems.at[1]),
    ]
    after_spec_ref[...] = spectrum((forward_high, forward_low), after_ref[...])
    for load in loads:
        load.wait()

    def step(row, sign):
        real = [grad_spec_ref[pl.ds(row, 8), col(b)] for b in range(GROUP)]
        real += [after_spec_ref[pl.ds(row, 8), col(b)] for b in range(REACH)]
        imag = [grad_spec_ref[pl.ds(row + LEN, 8), col(b)] for b in range(GROUP)]
        imag += [after_spec_ref[pl.ds(row + LEN, 8), col(b)] for b in range(REACH)]
        pairs = [
            (real[b] + sign * imag[b + 1], imag[b] - sign * real[b + 1]) for b in range(GROUP + REACH - 1)
        ]
        lag = [
            (lag_spec_ref[pl.ds(row, 8), col(d)], lag_spec_ref[pl.ds(row + LEN, 8), col(d)]) for d in range(REACH)
        ]
        for block in range(GROUP):
            total_real, total_imag = 0.0, 0.0
            for d in range(REACH):
                window = pairs[block + d]
                total_real += lag[d][0] * window[0] + lag[d][1] * window[1]
                total_imag += lag[d][0] * window[1] - lag[d][1] * window[0]
            product_ref[pl.ds(row, 8), col(block)] = total_real
            product_ref[pl.ds(row + LEN, 8), col(block)] = total_imag

    over_frequencies(step)
    result_ref[...] = invert((inverse_high, inverse_low), product_ref[...]).astype(BF16)


def pack_back(place_ref, result_ref, rounded_ref, *out_refs):
    for step in range(GROUP):
        there = lane((place_ref[0] + step) & (GROUP - 1))
        out_refs[step][:LEN, :] = result_ref[:, there]
        out_refs[step][LEN:, :] = rounded_ref[:, there]


def sum_terms(terms_ref, out_ref):
    groups = terms_ref.shape[0] // GROUP
    for place in range(GROUP):
        out_ref[:, col(place)] = sum(terms_ref[group * GROUP + place].astype(F32) for group in range(groups))


def finish(
    channels, place_ref, sums_ref, query_ref, key_ref, value_ref, cotangent_ref, stock_ref, class_ref, table_ref, *refs
):
    pieces, (normed_ref, grad_query_ref, grad_key_ref, grad_value_ref, lines_ref) = (
        refs[:GROUP], refs[GROUP:]
    )
    place = place_ref[0]
    half = GROUP // 2
    lines_ref[...] = row_lines(channels, sums_ref)
    lines = lines_ref[pl.ds(pl.multiple_of((place & 1) * LEN, LEN), LEN), :]
    number = lax.broadcasted_iota(jnp.int32, (LEN, GROUP), 1)
    inv = jnp.sum(jnp.where(number == place >> 1, lines, 0.0), axis=1, keepdims=True)
    mean = jnp.sum(jnp.where(number == half + (place >> 1), lines, 0.0), axis=1, keepdims=True)
    event_class = event_classes(stock_ref, class_ref)[:1]
    for step in range(GROUP):
        there = lane((place - step) & (GROUP - 1))
        piece = pieces[step]
        factor = modulation(event_class, table_ref[:, there])
        conv = piece[LEN:, :].astype(F32)
        normed = query_ref[:, there].astype(F32) * factor * conv * inv
        normed_ref[:, there] = normed.astype(BF16)
        grad_scaled = inv * (cotangent_ref[:, there].astype(F32) - normed * mean)
        grad_query_ref[:, there] = (grad_scaled * conv * factor).astype(BF16)
        grad_mixed = piece[:LEN, :].astype(F32)
        grad_key_ref[:, there] = (grad_mixed * value_ref[:, there].astype(F32)).astype(BF16)
        grad_value_ref[:, there] = (grad_mixed * key_ref[:, there].astype(F32)).astype(BF16)


def on_chip(shape, dtype):
    return pltpu.VMEM(shape, dtype)


def off_chip(shape, dtype):
    return pltpu.HBM(shape, dtype)


def near(value):
    return pltpu.with_memory_space_constraint(value, pltpu.VMEM)


def far(value):
    return pltpu.with_memory_space_constraint(value, pltpu.HBM)


def call(body, outs, *args, scalars=0, scratch=(), copies=0, left=(), manual=(), cost=1000):
    specs = [pl.BlockSpec(memory_space=pltpu.SMEM)] * scalars
    specs += [
        pl.BlockSpec(memory_space=pl.ANY if index in left else pltpu.VMEM) for index in range(scalars, len(args))
    ]
    moved = sum(a.size * a.dtype.itemsize for a in args)
    return pl.pallas_call(
        body,
        out_shape=list(outs),
        in_specs=specs,
        out_specs=[pl.BlockSpec(memory_space=pl.ANY if i in manual else pltpu.VMEM) for i in range(len(outs))],
        scratch_shapes=[pltpu.VMEM(shape, dtype) for shape, dtype in scratch]
        + ([pltpu.SemaphoreType.DMA(copies)] if copies else []),
        cost_estimate=pl.CostEstimate(flops=cost, bytes_accessed=moved, transcendentals=0),
        compiler_params=pltpu.CompilerParams(vmem_limit_bytes=20 << 20),
    )(*args)


def swap(pieces):
    return [pieces[0]] + [
        lax.ppermute(pieces[step], "j", [(i, (i + step) % GROUP) for i in range(GROUP)]) for step in range(1, GROUP)
    ]


def trade(value, mask, groups):
    return lax.ppermute(value, "g", [(i, i ^ mask) for i in range(groups)])


def shards(query_proj, key_proj, value_proj, filters, cotangent, stock_id, stock_class, cond_table):
    groups = lax.axis_size("g")
    parts = lax.axis_size("ch")
    near_groups = min(4, groups)
    far_groups = groups // near_groups
    lag_rows = filters.shape[0]
    wide = GROUP * LANES
    half = wide // 2
    place = jnp.stack([lax.axis_index("j"), lax.axis_index("g")]).astype(jnp.int32)
    tables = [jnp.asarray(t) for t in transform_tables()]
    far_tables = list(map(far, tables))
    stock_id, stock_class = far(stock_id[None, :]), far(stock_class[None, :])
    table = far(jnp.pad(cond_table, ((0, 16 - cond_table.shape[0]), (0, 0))))

    (sent,) = call(
        pack, [off_chip((GROUP, ROWS, LANES), BF16)], *map(far, (key_proj, value_proj, query_proj, cotangent)),
        stock_id, stock_class, manual=(0,), copies=(GROUP,), scratch=[((GROUP, ROWS, LANES), BF16)],
    )
    got = lax.all_to_all(sent, "j", 0, 0)
    lags = filters[None]
    lags = jnp.concatenate([lags] + [trade(lags, high * near_groups, groups) for high in range(1, far_groups)])
    lags = [lags] + [trade(lags, low, groups) for low in range(1, near_groups)]
    (lags,) = call(pack_lags, [off_chip((GROUP, groups * lag_rows, LANES), BF16)], *map(near, lags))
    got, lags = lax.optimization_barrier((got, lags))
    before = lax.ppermute(got[GROUP - REACH :, :LEN, :], "g", [(i, i + 1) for i in range(groups - 1)])
    got, lags = far(got), near(lax.all_to_all(lags, "j", 0, 0))
    own, gate = call(
        prepare, [off_chip((2 * LEN, wide), F32), off_chip((LEN, wide), F32)], place, table, got, *far_tables[:2],
        scalars=1, copies=(2,), manual=(0, 1), scratch=[((2 * LEN, wide), F32), ((LEN, wide), F32)],
        cost=2 * 4 * LEN * LEN * wide,
    )
    results = call(
        functools.partial(convolve, near_groups, far_groups),
        [
            on_chip((2 * LEN, wide), F32), on_chip((LEN, wide), F32), on_chip((GROUP, LEN, LANES), BF16),
            on_chip((2 * LEN, half), F32), on_chip((LEN, wide), F32),
        ]
        + [on_chip(t.shape, BF16) for t in tables]
        + [off_chip((2 * LEN, half), F32), off_chip((LEN, wide), BF16), off_chip((GROUP * parts, 8, 2 * LEN), F32)],
        place, far(own), far(gate), got, before, lags, *far_tables, scalars=1, copies=(9,), manual=(9, 10),
        left=(1, 2, 3, 6, 7, 8, 9),
        scratch=[((2 * LEN, half), F32), ((LEN, wide), BF16), ((2 * LEN, wide), F32), ((LEN, half), F32)],
        cost=2 * 10 * LEN * LEN * wide,
    )
    own, gate, upstream, before_spec, conv, *near_tables = map(near, results[:9])
    lag_spec, rounded, sums = results[9:]
    sums = lax.all_to_all(sums, ("j", "ch"), 0, 0)
    grad_conv, first = call(
        functools.partial(finish_norm, wide * parts), [on_chip((LEN, wide), BF16), on_chip((LEN, half), BF16)],
        far(sums), conv, gate, upstream,
    )
    after = lax.ppermute(first, "g", [(i, i - 1) for i in range(1, groups)])
    grad_spec, terms = call(
        filter_terms, [off_chip((2 * LEN, wide), F32), off_chip((REACH, LEN, LANES), BF16)],
        near(grad_conv), own, before_spec, *near_tables, copies=(1,), manual=(0,),
        scratch=[((2 * LEN, half), F32), ((2 * LEN, wide), F32)],
        cost=2 * 7 * LEN * LEN * wide,
    )
    (back,) = call(
        correlate_back, [on_chip((LEN, wide), BF16)], far(grad_spec), far(lag_spec), after, *far_tables, left=(0, 1),
        copies=(2,),
        scratch=[((2 * LEN, half), F32), ((2 * LEN, wide), F32), ((2 * LEN, wide), F32), ((2 * LEN, half), F32)],
        cost=2 * 8 * LEN * LEN * wide,
    )
    back = call(pack_back, [on_chip((2 * LEN, LANES), BF16)] * GROUP, place, near(back), rounded, scalars=1)
    back = swap(back)
    terms = lax.all_to_all(terms.reshape(groups * GROUP, lag_rows, LANES), ("g", "j"), 0, 0)
    (grad_filter,) = call(sum_terms, [off_chip((lag_rows, wide), F32)], terms)
    outs = call(
        functools.partial(finish, wide * parts),
        [off_chip((LEN, wide), BF16)] * 4,
        place, far(sums), *map(near, (query_proj, key_proj, value_proj, cotangent)), stock_id, stock_class, table,
        *map(near, back), scalars=1, scratch=[((2 * LEN, GROUP), F32)],
    )
    return *outs, grad_filter


def solution(mesh):
    ctx, ch = mesh.devices.shape
    inner = Mesh(mesh.devices.reshape(ctx // GROUP, GROUP, ch), ("g", "j", "ch"))
    rows = ("g", "j")
    return jax.shard_map(
        shards,
        mesh=inner,
        in_specs=(P(rows, "ch"),) * 5 + (P(rows), P(), P(None, "ch")),
        out_specs=(P(rows, "ch"),) * 5,
        check_vma=False,
    )
```

```python
import functools

import jax
import jax.numpy as jnp
import numpy as np
import ml_dtypes
from jax import lax
from jax.experimental import pallas as pl
from jax.experimental.pallas import tpu as pltpu
from jax.sharding import Mesh, PartitionSpec as P

GROUP = 8
REACH = 4
LEN = 256
LANES = 128
EPSILON = 1e-05
F32 = jnp.float32
BF16 = jnp.bfloat16


def split_table(table):
    high = table.astype(np.float32).astype(ml_dtypes.bfloat16)
    low = (table - high.astype(np.float64)).astype(ml_dtypes.bfloat16)
    return high, low


def transform_tables():
    number = np.concatenate([np.arange(0, LEN, 2), np.arange(1, LEN, 2)])
    angles = np.pi * ((2 * number[:, None] + 1) * np.arange(LEN)[None, :] % (4 * LEN)) / (2 * LEN)
    forward = np.concatenate([np.cos(angles), -np.sin(angles)], axis=0)
    return (*split_table(forward), *split_table(forward.T / LEN))


def dot(left, right):
    return jnp.dot(left, right, preferred_element_type=F32)


def halves(value):
    high = value.astype(BF16)
    return high, (value - high.astype(F32)).astype(BF16)


def lane(index):
    return pl.ds(pl.multiple_of(index * LANES, LANES), LANES)


def col(index):
    return slice(index * LANES, (index + 1) * LANES)


def event_classes(stock_ref, class_ref):
    stocks = class_ref.shape[1]
    hits = (lax.broadcasted_iota(jnp.int32, (stocks, LEN), 0) == stock_ref[...]).astype(F32).astype(BF16)
    classes = jnp.broadcast_to(class_ref[...].astype(F32), (8, stocks)).astype(BF16)
    return dot(classes, hits)


def modulation(event_class, table):
    high = table.astype(BF16)
    mid = (table - high.astype(F32)).astype(BF16)
    low = (table - high.astype(F32) - mid.astype(F32)).astype(BF16)
    number = lax.broadcasted_iota(jnp.int32, (table.shape[0], LEN), 0).astype(F32)
    hits = jnp.transpose((number == event_class).astype(F32)).astype(BF16)
    return 1.0 + (dot(hits, high) + dot(hits, mid) + dot(hits, low))


def copy_out(source, target, sem):
    copy = pltpu.make_async_copy(source, target, sem)
    copy.start()
    return copy


QUERY, UPSTREAM, CLASS, ROWS = LEN, 2 * LEN, 3 * LEN, 3 * LEN + 16


def pack(key_ref, value_ref, query_ref, cotangent_ref, stock_ref, class_ref, out_hbm, out_ref, sems):
    event_class = event_classes(stock_ref, class_ref).astype(BF16)
    copies = []
    for place in range(GROUP):
        product = key_ref[:, col(place)].astype(F32) * value_ref[:, col(place)].astype(F32)
        out_ref[place, :LEN, :] = product.astype(BF16)
        out_ref[place, QUERY:UPSTREAM, :] = query_ref[:, col(place)]
        out_ref[place, UPSTREAM:CLASS, :] = cotangent_ref[:, col(place)]
        out_ref[place, CLASS : CLASS + 8, :] = event_class[:, :LANES]
        out_ref[place, CLASS + 8 :, :] = event_class[:, LANES:]
        copies.append(copy_out(out_ref.at[place], out_hbm.at[place], sems.at[place]))
    for copy in copies:
        copy.wait()


def pack_lags(*refs):
    out_ref, first = refs[-1], 0
    for lags_ref in refs[:-1]:
        rows = lags_ref.shape[1]
        for high in range(lags_ref.shape[0]):
            for place in range(GROUP):
                out_ref[place, first : first + rows, :] = lags_ref[high, :, col(place)]
            first += rows


def spectrum(forward, rows):
    return dot(forward[0][...], rows) + dot(forward[1][...], rows)


def invert(inverse, spec):
    high, low = halves(spec)
    return dot(inverse[0][...], high) + (dot(inverse[0][...], low) + dot(inverse[1][...], high))


def over_frequencies(step):
    for half in range(2):
        @pl.loop(0, LEN // 16)
        def _(chunk):
            step(pl.multiple_of(half * (LEN // 2) + chunk * 8, 8), 1.0 - 2.0 * half)


def windows(real, imag, sign):
    pairs = {}
    for block in range(1, len(real)):
        pairs[block] = (real[block] - sign * imag[block - 1], imag[block] + sign * real[block - 1])
    return pairs


def read_blocks(own_ref, before_ref, row):
    real = [before_ref[pl.ds(row, 8), col(block)] for block in range(REACH)]
    real += [own_ref[pl.ds(row, 8), col(block)] for block in range(GROUP)]
    imag = [before_ref[pl.ds(row + LEN, 8), col(block)] for block in range(REACH)]
    imag += [own_ref[pl.ds(row + LEN, 8), col(block)] for block in range(GROUP)]
    return real, imag


def prepare(place_ref, table_ref, got_ref, forward_high, forward_low, own_out, gate_out, own_ref, gate_ref, sems):
    rows = jnp.concatenate([got_ref[b, :LEN, :] for b in range(GROUP)], axis=1)
    own_ref[...] = spectrum((forward_high, forward_low), rows)
    copies = [copy_out(own_ref, own_out, sems.at[0])]
    table = table_ref[:, lane(place_ref[0])]
    for block in range(GROUP):
        classes = got_ref[block, CLASS:, :].astype(F32)
        event_class = jnp.concatenate([classes[:1], classes[8:9]], axis=1)
        gate_ref[:, col(block)] = got_ref[block, QUERY:UPSTREAM, :].astype(F32) * modulation(event_class, table)
    copies.append(copy_out(gate_ref, gate_out, sems.at[1]))
    for copy in copies:
        copy.wait()


def convolve(near_groups, far_groups, place_ref, own_hbm, gate_hbm, got_hbm, before_ref, lags_ref, *refs):
    own_ref, gate_ref, upstream_ref, before_spec_ref, conv_ref = refs[4:9]
    forward, inverse = refs[9:11], refs[11:13]
    lag_spec_hbm, rounded_hbm, sums_ref, lag_spec_ref, rounded_ref, product_ref, sorted_ref, sems = refs[13:]
    tables = [copy_out(refs[i], refs[9 + i], sems.at[5 + i]) for i in range(4)]
    loads = [
        copy_out(own_hbm, own_ref, sems.at[0]),
        copy_out(gate_hbm, gate_ref, sems.at[1]),
        copy_out(got_hbm.at[:, UPSTREAM:CLASS, :], upstream_ref, sems.at[2]),
    ]
    group = place_ref[1]
    tables[0].wait()
    tables[1].wait()
    before_spec_ref[...] = spectrum(forward, jnp.concatenate([before_ref[b] for b in range(REACH)], axis=1))
    rows = lags_ref.shape[1] // (near_groups * far_groups)
    for low in range(near_groups):
        for high in range(far_groups):
            at = (low * far_groups + high) * rows
            first = (group ^ (high * near_groups + low)) * (GROUP * rows)
            row = pl.multiple_of(first & (LEN - 1), GROUP * rows)
            piece = lags_ref[:, at : at + rows, :].astype(F32).reshape(GROUP * rows, LANES)
            sorted_ref[pl.ds(row, GROUP * rows), lane(first // LEN)] = piece
    lag_spec_ref[...] = spectrum(forward, sorted_ref[...].astype(BF16))
    copies = [copy_out(lag_spec_ref, lag_spec_hbm, sems.at[4])]
    loads[0].wait()

    def step(row, sign):
        real, imag = read_blocks(own_ref, before_spec_ref, row)
        pairs = windows(real, imag, sign)
        lag = [
            (lag_spec_ref[pl.ds(row, 8), col(d)], lag_spec_ref[pl.ds(row + LEN, 8), col(d)]) for d in range(REACH)
        ]
        for block in range(GROUP):
            total_real, total_imag = 0.0, 0.0
            for d in range(REACH):
                window = pairs[REACH + block - d]
                total_real += lag[d][0] * window[0] - lag[d][1] * window[1]
                total_imag += lag[d][0] * window[1] + lag[d][1] * window[0]
            product_ref[pl.ds(row, 8), col(block)] = total_real
            product_ref[pl.ds(row + LEN, 8), col(block)] = total_imag

    over_frequencies(step)
    tables[2].wait()
    tables[3].wait()
    conv = invert(inverse, product_ref[...])
    conv_ref[...] = conv
    rounded_ref[...] = conv.astype(BF16)
    copies.append(copy_out(rounded_ref, rounded_hbm, sems.at[3]))
    loads[1].wait()
    loads[2].wait()
    ones = jnp.ones((8, LANES), BF16)

    def channel_sum(value):
        contract = (((1,), (1,)), ((), ()))
        return sum(lax.dot_general(ones, part, contract, preferred_element_type=F32) for part in halves(value))[:1]

    lines = [[], []]
    for block in range(GROUP):
        scaled = gate_ref[:, col(block)] * conv[:, col(block)]
        lines[0].append(channel_sum(scaled * scaled))
        lines[1].append(channel_sum(scaled * upstream_ref[block].astype(F32)))
    for index in range(2):
        for pair in range(GROUP // 2):
            both = jnp.concatenate(lines[index][2 * pair : 2 * pair + 2], axis=1)
            line = index * (GROUP // 2) + pair
            for peer in range(sums_ref.shape[0]):
                sums_ref[peer, line : line + 1, :] = both
    for copy in copies:
        copy.wait()


def row_lines(channels, sums_ref):
    total = jnp.sum(sums_ref[...], axis=0)
    half = GROUP // 2
    inv_rms = lax.rsqrt(total[:half] / channels + EPSILON)
    return jnp.transpose(jnp.concatenate([inv_rms, total[half:] * inv_rms / channels], axis=0))


def finish_norm(channels, sums_ref, conv_ref, gate_ref, upstream_ref, grad_ref, first_ref):
    lines = row_lines(channels, sums_ref)
    half = GROUP // 2
    for block in range(GROUP):
        rows = slice((block % 2) * LEN, (block % 2 + 1) * LEN)
        inv = lines[rows, block // 2 : block // 2 + 1]
        mean = lines[rows, half + block // 2 : half + block // 2 + 1]
        gate = gate_ref[:, col(block)]
        normed = gate * conv_ref[:, col(block)] * inv
        grad_conv = (inv * (upstream_ref[block].astype(F32) - normed * mean) * gate).astype(BF16)
        grad_ref[:, col(block)] = grad_conv
        if block < REACH:
            first_ref[:, col(block)] = grad_conv


def filter_terms(
    grad_ref, own_ref, before_ref, forward_high, forward_low, inverse_high, inverse_low, grad_spec_hbm, terms_ref,
    product_ref, grad_spec_ref, sems,
):
    grad_spec_ref[...] = spectrum((forward_high, forward_low), grad_ref[...])
    copy = copy_out(grad_spec_ref, grad_spec_hbm, sems.at[0])

    def step(row, sign):
        real, imag = read_blocks(own_ref, before_ref, row)
        pairs = windows(real, imag, sign)
        grads = [
            (grad_spec_ref[pl.ds(row, 8), col(b)], grad_spec_ref[pl.ds(row + LEN, 8), col(b)]) for b in range(GROUP)
        ]
        for d in range(REACH):
            total_real, total_imag = 0.0, 0.0
            for block in range(GROUP):
                window = pairs[REACH + block - d]
                total_real += grads[block][0] * window[0] + grads[block][1] * window[1]
                total_imag += grads[block][1] * window[0] - grads[block][0] * window[1]
            product_ref[pl.ds(row, 8), col(d)] = total_real
            product_ref[pl.ds(row + LEN, 8), col(d)] = total_imag

    over_frequencies(step)
    terms = invert((inverse_high, inverse_low), product_ref[...])
    for d in range(REACH):
        terms_ref[d] = terms[:, col(d)].astype(BF16)
    copy.wait()


def correlate_back(place_ref, *refs):
    tables_hbm, (grad_spec_hbm, lag_spec_hbm, rounded_hbm, after_ref) = refs[:4], refs[4:8]
    out_refs, tables = refs[8 : 8 + GROUP], refs[8 + GROUP : 12 + GROUP]
    result_ref, after_spec_ref, product_ref, grad_spec_ref, lag_spec_ref, sems = refs[12 + GROUP :]
    place = place_ref[0]
    table_loads = [copy_out(tables_hbm[i], tables[i], sems.at[i]) for i in range(2)]
    loads = [
        copy_out(grad_spec_hbm, grad_spec_ref, sems.at[4]),
        copy_out(lag_spec_hbm, lag_spec_ref, sems.at[5]),
    ]
    table_loads += [copy_out(tables_hbm[i], tables[i], sems.at[i]) for i in range(2, 4)]
    copies = [
        copy_out(
            rounded_hbm.at[:, lane((place + step_number) & (GROUP - 1))],
            out_refs[step_number].at[LEN:, :],
            sems.at[6 + step_number],
        )
        for step_number in range(GROUP)
    ]
    (forward_high, forward_low), (inverse_high, inverse_low) = tables[:2], tables[2:]
    table_loads[0].wait()
    table_loads[1].wait()
    after_spec_ref[...] = spectrum((forward_high, forward_low), after_ref[...])
    for load in loads:
        load.wait()

    def step(row, sign):
        real = [grad_spec_ref[pl.ds(row, 8), col(b)] for b in range(GROUP)]
        real += [after_spec_ref[pl.ds(row, 8), col(b)] for b in range(REACH)]
        imag = [grad_spec_ref[pl.ds(row + LEN, 8), col(b)] for b in range(GROUP)]
        imag += [after_spec_ref[pl.ds(row + LEN, 8), col(b)] for b in range(REACH)]
        pairs = [
            (real[b] + sign * imag[b + 1], imag[b] - sign * real[b + 1]) for b in range(GROUP + REACH - 1)
        ]
        lag = [
            (lag_spec_ref[pl.ds(row, 8), col(d)], lag_spec_ref[pl.ds(row + LEN, 8), col(d)]) for d in range(REACH)
        ]
        for block in range(GROUP):
            total_real, total_imag = 0.0, 0.0
            for d in range(REACH):
                window = pairs[block + d]
                total_real += lag[d][0] * window[0] + lag[d][1] * window[1]
                total_imag += lag[d][0] * window[1] - lag[d][1] * window[0]
            product_ref[pl.ds(row, 8), col(block)] = total_real
            product_ref[pl.ds(row + LEN, 8), col(block)] = total_imag

    over_frequencies(step)
    table_loads[2].wait()
    table_loads[3].wait()
    result_ref[...] = invert((inverse_high, inverse_low), product_ref[...]).astype(BF16)
    for step_number in range(GROUP):
        out_refs[step_number][:LEN, :] = result_ref[:, lane((place + step_number) & (GROUP - 1))]
    for copy in copies:
        copy.wait()


def sum_terms(terms_ref, out_ref):
    groups = terms_ref.shape[0] // GROUP
    for place in range(GROUP):
        out_ref[:, col(place)] = sum(terms_ref[group * GROUP + place].astype(F32) for group in range(groups))


def finish(
    channels, place_ref, sums_ref, query_ref, key_ref, value_ref, cotangent_ref, stock_ref, class_ref, table_ref, *refs
):
    pieces = refs[:GROUP]
    normed_ref, grad_query_ref, grad_key_ref, grad_value_ref, factor_ref, lines_ref = refs[GROUP:]
    place = place_ref[0]
    half = GROUP // 2
    lines_ref[...] = row_lines(channels, sums_ref)
    lines = lines_ref[pl.ds(pl.multiple_of((place & 1) * LEN, LEN), LEN), :]
    number = lax.broadcasted_iota(jnp.int32, (LEN, GROUP), 1)
    inv = jnp.sum(jnp.where(number == place >> 1, lines, 0.0), axis=1, keepdims=True)
    mean = jnp.sum(jnp.where(number == half + (place >> 1), lines, 0.0), axis=1, keepdims=True)
    factor_ref[...] = modulation(event_classes(stock_ref, class_ref)[:1], table_ref[...])
    for step in range(GROUP):
        there = lane((place - step) & (GROUP - 1))
        piece = pieces[step]
        grad_mixed = piece[:LEN, :].astype(F32)
        grad_key_ref[:, there] = (grad_mixed * value_ref[:, there].astype(F32)).astype(BF16)
        grad_value_ref[:, there] = (grad_mixed * key_ref[:, there].astype(F32)).astype(BF16)
        factor = factor_ref[:, there]
        conv = piece[LEN:, :].astype(F32)
        normed = query_ref[:, there].astype(F32) * factor * conv * inv
        normed_ref[:, there] = normed.astype(BF16)
        grad_scaled = inv * (cotangent_ref[:, there].astype(F32) - normed * mean)
        grad_query_ref[:, there] = (grad_scaled * conv * factor).astype(BF16)


def on_chip(shape, dtype):
    return pltpu.VMEM(shape, dtype)


def off_chip(shape, dtype):
    return pltpu.HBM(shape, dtype)


def near(value):
    return pltpu.with_memory_space_constraint(value, pltpu.VMEM)


def far(value):
    return pltpu.with_memory_space_constraint(value, pltpu.HBM)


def call(body, outs, *args, scalars=0, scratch=(), copies=0, left=(), manual=(), cost=1000):
    specs = [pl.BlockSpec(memory_space=pltpu.SMEM)] * scalars
    specs += [
        pl.BlockSpec(memory_space=pl.ANY if index in left else pltpu.VMEM) for index in range(scalars, len(args))
    ]
    moved = sum(a.size * a.dtype.itemsize for a in args)
    return pl.pallas_call(
        body,
        out_shape=list(outs),
        in_specs=specs,
        out_specs=[pl.BlockSpec(memory_space=pl.ANY if i in manual else pltpu.VMEM) for i in range(len(outs))],
        scratch_shapes=[pltpu.VMEM(shape, dtype) for shape, dtype in scratch]
        + ([pltpu.SemaphoreType.DMA(copies)] if copies else []),
        cost_estimate=pl.CostEstimate(flops=cost, bytes_accessed=moved, transcendentals=0),
        compiler_params=pltpu.CompilerParams(vmem_limit_bytes=20 << 20),
    )(*args)


def swap(pieces):
    return [pieces[0]] + [
        lax.ppermute(pieces[step], "j", [(i, (i + step) % GROUP) for i in range(GROUP)]) for step in range(1, GROUP)
    ]


def trade(value, mask, groups):
    return lax.ppermute(value, "g", [(i, i ^ mask) for i in range(groups)])


def shards(query_proj, key_proj, value_proj, filters, cotangent, stock_id, stock_class, cond_table):
    groups = lax.axis_size("g")
    parts = lax.axis_size("ch")
    near_groups = min(4, groups)
    far_groups = groups // near_groups
    lag_rows = filters.shape[0]
    wide = GROUP * LANES
    half = wide // 2
    place = jnp.stack([lax.axis_index("j"), lax.axis_index("g")]).astype(jnp.int32)
    tables = [jnp.asarray(t) for t in transform_tables()]
    far_tables = list(map(far, tables))
    stock_id, stock_class = far(stock_id[None, :]), far(stock_class[None, :])
    table = far(jnp.pad(cond_table, ((0, 16 - cond_table.shape[0]), (0, 0))))

    (sent,) = call(
        pack, [off_chip((GROUP, ROWS, LANES), BF16)], *map(far, (key_proj, value_proj, query_proj, cotangent)),
        stock_id, stock_class, manual=(0,), copies=(GROUP,), scratch=[((GROUP, ROWS, LANES), BF16)],
    )
    got = lax.all_to_all(sent, "j", 0, 0)
    lags = filters[None]
    lags = jnp.concatenate([lags] + [trade(lags, high * near_groups, groups) for high in range(1, far_groups)])
    lags = [lags] + [trade(lags, low, groups) for low in range(1, near_groups)]
    (lags,) = call(pack_lags, [off_chip((GROUP, groups * lag_rows, LANES), BF16)], *map(near, lags))
    got, lags = lax.optimization_barrier((got, lags))
    before = lax.ppermute(got[GROUP - REACH :, :LEN, :], "g", [(i, i + 1) for i in range(groups - 1)])
    got, lags = far(got), near(lax.all_to_all(lags, "j", 0, 0))
    own, gate = call(
        prepare, [off_chip((2 * LEN, wide), F32), off_chip((LEN, wide), F32)], place, table, got, *far_tables[:2],
        scalars=1, copies=(2,), manual=(0, 1), scratch=[((2 * LEN, wide), F32), ((LEN, wide), F32)],
        cost=2 * 4 * LEN * LEN * wide,
    )
    results = call(
        functools.partial(convolve, near_groups, far_groups),
        [
            on_chip((2 * LEN, wide), F32), on_chip((LEN, wide), F32), on_chip((GROUP, LEN, LANES), BF16),
            on_chip((2 * LEN, half), F32), on_chip((LEN, wide), F32),
        ]
        + [on_chip(t.shape, BF16) for t in tables]
        + [off_chip((2 * LEN, half), F32), off_chip((LEN, wide), BF16), on_chip((GROUP * parts, 8, 2 * LEN), F32)],
        place, far(own), far(gate), got, before, lags, *far_tables, scalars=1, copies=(9,), manual=(9, 10),
        left=(1, 2, 3, 6, 7, 8, 9),
        scratch=[((2 * LEN, half), F32), ((LEN, wide), BF16), ((2 * LEN, wide), F32), ((LEN, half), F32)],
        cost=2 * 10 * LEN * LEN * wide,
    )
    own, gate, upstream, before_spec, conv, *near_tables = map(near, results[:9])
    lag_spec, rounded, sums = results[9:]
    sums = lax.all_to_all(sums, ("j", "ch"), 0, 0)
    grad_conv, first = call(
        functools.partial(finish_norm, wide * parts), [on_chip((LEN, wide), BF16), on_chip((LEN, half), BF16)],
        near(sums), conv, gate, upstream,
    )
    after = lax.ppermute(first, "g", [(i, i - 1) for i in range(1, groups)])
    grad_spec, terms = call(
        filter_terms, [off_chip((2 * LEN, wide), F32), off_chip((REACH, LEN, LANES), BF16)],
        near(grad_conv), own, before_spec, *near_tables, copies=(1,), manual=(0,),
        scratch=[((2 * LEN, half), F32), ((2 * LEN, wide), F32)],
        cost=2 * 7 * LEN * LEN * wide,
    )
    back = call(
        correlate_back, [on_chip((2 * LEN, LANES), BF16)] * GROUP, place, *far_tables, far(grad_spec), far(lag_spec),
        far(rounded), after, scalars=1, left=range(1, 8), copies=(6 + GROUP,),
        scratch=[(t.shape, BF16) for t in tables]
        + [
            ((LEN, wide), BF16), ((2 * LEN, half), F32), ((2 * LEN, wide), F32), ((2 * LEN, wide), F32),
            ((2 * LEN, half), F32),
        ],
        cost=2 * 8 * LEN * LEN * wide,
    )
    back = swap(back)
    terms = lax.all_to_all(terms.reshape(groups * GROUP, lag_rows, LANES), ("g", "j"), 0, 0)
    (grad_filter,) = call(sum_terms, [off_chip((lag_rows, wide), F32)], terms)
    outs = call(
        functools.partial(finish, wide * parts),
        [off_chip((LEN, wide), BF16)] * 4,
        place, far(sums), *map(near, (query_proj, key_proj, value_proj, cotangent)), stock_id, stock_class, table,
        *map(near, back), scalars=1, scratch=[((LEN, wide), F32), ((2 * LEN, GROUP), F32)],
    )
    return *outs, grad_filter


def solution(mesh):
    ctx, ch = mesh.devices.shape
    inner = Mesh(mesh.devices.reshape(ctx // GROUP, GROUP, ch), ("g", "j", "ch"))
    rows = ("g", "j")
    return jax.shard_map(
        shards,
        mesh=inner,
        in_specs=(P(rows, "ch"),) * 5 + (P(rows), P(), P(None, "ch")),
        out_specs=(P(rows, "ch"),) * 5,
        check_vma=False,
    )
```

```python
import functools

import jax
import jax.numpy as jnp
import numpy as np
import ml_dtypes
from jax import lax
from jax.experimental import pallas as pl
from jax.experimental.pallas import tpu as pltpu
from jax.sharding import Mesh, PartitionSpec as P

GROUP = 8
REACH = 4
LEN = 256
LANES = 128
EPSILON = 1e-05
F32 = jnp.float32
BF16 = jnp.bfloat16


def split_table(table):
    high = table.astype(np.float32).astype(ml_dtypes.bfloat16)
    low = (table - high.astype(np.float64)).astype(ml_dtypes.bfloat16)
    return high, low


def transform_tables():
    number = np.concatenate([np.arange(0, LEN, 2), np.arange(1, LEN, 2)])
    angles = np.pi * ((2 * number[:, None] + 1) * np.arange(LEN)[None, :] % (4 * LEN)) / (2 * LEN)
    forward = np.concatenate([np.cos(angles), -np.sin(angles)], axis=0)
    return (*split_table(forward), *split_table(forward.T / LEN))


def dot(left, right):
    return jnp.dot(left, right, preferred_element_type=F32)


def halves(value):
    high = value.astype(BF16)
    return high, (value - high.astype(F32)).astype(BF16)


def lane(index):
    return pl.ds(pl.multiple_of(index * LANES, LANES), LANES)


def col(index):
    return slice(index * LANES, (index + 1) * LANES)


def event_classes(stock_ref, class_ref):
    stocks = class_ref.shape[1]
    hits = (lax.broadcasted_iota(jnp.int32, (stocks, LEN), 0) == stock_ref[...]).astype(F32).astype(BF16)
    classes = jnp.broadcast_to(class_ref[...].astype(F32), (8, stocks)).astype(BF16)
    return dot(classes, hits)


def modulation(event_class, table):
    high = table.astype(BF16)
    mid = (table - high.astype(F32)).astype(BF16)
    low = (table - high.astype(F32) - mid.astype(F32)).astype(BF16)
    number = lax.broadcasted_iota(jnp.int32, (table.shape[0], LEN), 0).astype(F32)
    hits = jnp.transpose((number == event_class).astype(F32)).astype(BF16)
    return 1.0 + (dot(hits, high) + dot(hits, mid) + dot(hits, low))


def copy_out(source, target, sem):
    copy = pltpu.make_async_copy(source, target, sem)
    copy.start()
    return copy


QUERY, UPSTREAM, CLASS, ROWS = LEN, 2 * LEN, 3 * LEN, 3 * LEN + 16


def pack(key_ref, value_ref, query_ref, cotangent_ref, stock_ref, class_ref, out_hbm, out_ref, event_ref, sems):
    copies = []
    for place in range(GROUP):
        product = key_ref[:, col(place)].astype(F32) * value_ref[:, col(place)].astype(F32)
        out_ref[place, :LEN, :] = product.astype(BF16)
        out_ref[place, QUERY:UPSTREAM, :] = query_ref[:, col(place)]
        out_ref[place, UPSTREAM:, :] = cotangent_ref[:, col(place)]
        copies.append(copy_out(out_ref.at[place], out_hbm.at[place, :CLASS, :], sems.at[place]))
    event_class = event_classes(stock_ref, class_ref).astype(BF16)
    event_ref[...] = jnp.concatenate([event_class[:, :LANES], event_class[:, LANES:]], axis=0)
    for place in range(GROUP):
        copies.append(copy_out(event_ref, out_hbm.at[place, CLASS:, :], sems.at[GROUP + place]))
    for copy in copies:
        copy.wait()


def pack_lags(*refs):
    out_ref, first = refs[-1], 0
    for lags_ref in refs[:-1]:
        rows = lags_ref.shape[1]
        for high in range(lags_ref.shape[0]):
            for place in range(GROUP):
                out_ref[place, first : first + rows, :] = lags_ref[high, :, col(place)]
            first += rows


def spectrum(forward, rows):
    return dot(forward[0][...], rows) + dot(forward[1][...], rows)


def invert(inverse, spec):
    high, low = halves(spec)
    return dot(inverse[0][...], high) + (dot(inverse[0][...], low) + dot(inverse[1][...], high))


def over_frequencies(step):
    for half in range(2):
        @pl.loop(0, LEN // 16)
        def _(chunk):
            step(pl.multiple_of(half * (LEN // 2) + chunk * 8, 8), 1.0 - 2.0 * half)


def windows(real, imag, sign):
    pairs = {}
    for block in range(1, len(real)):
        pairs[block] = (real[block] - sign * imag[block - 1], imag[block] + sign * real[block - 1])
    return pairs


def read_blocks(own_ref, before_ref, row):
    real = [before_ref[pl.ds(row, 8), col(block)] for block in range(REACH)]
    real += [own_ref[pl.ds(row, 8), col(block)] for block in range(GROUP)]
    imag = [before_ref[pl.ds(row + LEN, 8), col(block)] for block in range(REACH)]
    imag += [own_ref[pl.ds(row + LEN, 8), col(block)] for block in range(GROUP)]
    return real, imag


def prepare(
    place_ref, table_ref, got_ref, stock_ref, class_ref, forward_high, forward_low, own_out, gate_out, factor_out, own_ref,
    gate_ref, factor_ref, sems,
):
    rows = jnp.concatenate([got_ref[b, :LEN, :] for b in range(GROUP)], axis=1)
    own_ref[...] = spectrum((forward_high, forward_low), rows)
    copies = [copy_out(own_ref, own_out, sems.at[0])]
    table = table_ref[:, lane(place_ref[0])]
    for block in range(GROUP):
        classes = got_ref[block, CLASS:, :].astype(F32)
        event_class = jnp.concatenate([classes[:1], classes[8:9]], axis=1)
        gate_ref[:, col(block)] = got_ref[block, QUERY:UPSTREAM, :].astype(F32) * modulation(event_class, table)
    copies.append(copy_out(gate_ref, gate_out, sems.at[1]))
    factor_ref[...] = modulation(event_classes(stock_ref, class_ref)[:1], table_ref[...])
    copies.append(copy_out(factor_ref, factor_out, sems.at[2]))
    for copy in copies:
        copy.wait()


def convolve(near_groups, far_groups, place_ref, own_hbm, gate_hbm, got_hbm, before_ref, lags_ref, *refs):
    own_ref, gate_ref, upstream_ref, before_spec_ref, conv_ref = refs[4:9]
    forward, inverse = refs[9:11], refs[11:13]
    lag_spec_hbm, rounded_hbm, sums_ref, lag_spec_ref, rounded_ref, product_ref, sorted_ref, sems = refs[13:]
    tables = [copy_out(refs[i], refs[9 + i], sems.at[5 + i]) for i in range(2)]
    loads = [copy_out(own_hbm, own_ref, sems.at[0])]
    tables += [copy_out(refs[i], refs[9 + i], sems.at[5 + i]) for i in range(2, 4)]
    loads += [
        copy_out(gate_hbm, gate_ref, sems.at[1]),
        copy_out(got_hbm.at[:, UPSTREAM:CLASS, :], upstream_ref, sems.at[2]),
    ]
    group = place_ref[1]
    tables[0].wait()
    tables[1].wait()
    before_spec_ref[...] = spectrum(forward, jnp.concatenate([before_ref[b] for b in range(REACH)], axis=1))
    rows = lags_ref.shape[1] // (near_groups * far_groups)
    for low in range(near_groups):
        for high in range(far_groups):
            at = (low * far_groups + high) * rows
            first = (group ^ (high * near_groups + low)) * (GROUP * rows)
            row = pl.multiple_of(first & (LEN - 1), GROUP * rows)
            piece = lags_ref[:, at : at + rows, :].astype(F32).reshape(GROUP * rows, LANES)
            sorted_ref[pl.ds(row, GROUP * rows), lane(first // LEN)] = piece
    lag_spec_ref[...] = spectrum(forward, sorted_ref[...].astype(BF16))
    copies = [copy_out(lag_spec_ref, lag_spec_hbm, sems.at[4])]
    loads[0].wait()

    def step(row, sign):
        real, imag = read_blocks(own_ref, before_spec_ref, row)
        pairs = windows(real, imag, sign)
        lag = [
            (lag_spec_ref[pl.ds(row, 8), col(d)], lag_spec_ref[pl.ds(row + LEN, 8), col(d)]) for d in range(REACH)
        ]
        for block in range(GROUP):
            total_real, total_imag = 0.0, 0.0
            for d in range(REACH):
                window = pairs[REACH + block - d]
                total_real += lag[d][0] * window[0] - lag[d][1] * window[1]
                total_imag += lag[d][0] * window[1] + lag[d][1] * window[0]
            product_ref[pl.ds(row, 8), col(block)] = total_real
            product_ref[pl.ds(row + LEN, 8), col(block)] = total_imag

    over_frequencies(step)
    tables[2].wait()
    tables[3].wait()
    conv = invert(inverse, product_ref[...])
    conv_ref[...] = conv
    rounded_ref[...] = conv.astype(BF16)
    copies.append(copy_out(rounded_ref, rounded_hbm, sems.at[3]))
    loads[1].wait()
    loads[2].wait()
    ones = jnp.ones((8, LANES), BF16)

    def channel_sum(value):
        contract = (((1,), (1,)), ((), ()))
        return sum(lax.dot_general(ones, part, contract, preferred_element_type=F32) for part in halves(value))[:1]

    lines = [[], []]
    for block in range(GROUP):
        scaled = gate_ref[:, col(block)] * conv[:, col(block)]
        lines[0].append(channel_sum(scaled * scaled))
        lines[1].append(channel_sum(scaled * upstream_ref[block].astype(F32)))
    for index in range(2):
        for pair in range(GROUP // 2):
            both = jnp.concatenate(lines[index][2 * pair : 2 * pair + 2], axis=1)
            line = index * (GROUP // 2) + pair
            for peer in range(sums_ref.shape[0]):
                sums_ref[peer, line : line + 1, :] = both
    for copy in copies:
        copy.wait()


def row_lines(channels, sums_ref):
    total = jnp.sum(sums_ref[...], axis=0)
    half = GROUP // 2
    inv_rms = lax.rsqrt(total[:half] / channels + EPSILON)
    return jnp.transpose(jnp.concatenate([inv_rms, total[half:] * inv_rms / channels], axis=0))


def finish_norm(channels, sums_ref, conv_ref, gate_ref, upstream_ref, grad_ref, first_ref):
    lines = row_lines(channels, sums_ref)
    half = GROUP // 2
    for block in range(GROUP):
        rows = slice((block % 2) * LEN, (block % 2 + 1) * LEN)
        inv = lines[rows, block // 2 : block // 2 + 1]
        mean = lines[rows, half + block // 2 : half + block // 2 + 1]
        gate = gate_ref[:, col(block)]
        normed = gate * conv_ref[:, col(block)] * inv
        grad_conv = (inv * (upstream_ref[block].astype(F32) - normed * mean) * gate).astype(BF16)
        grad_ref[:, col(block)] = grad_conv
        if block < REACH:
            first_ref[:, col(block)] = grad_conv


def filter_terms(
    grad_ref, own_ref, before_ref, forward_high, forward_low, inverse_high, inverse_low, grad_spec_hbm, terms_ref,
    product_ref, grad_spec_ref, sems,
):
    grad_spec_ref[...] = spectrum((forward_high, forward_low), grad_ref[...])
    copy = copy_out(grad_spec_ref, grad_spec_hbm, sems.at[0])

    def step(row, sign):
        real, imag = read_blocks(own_ref, before_ref, row)
        pairs = windows(real, imag, sign)
        grads = [
            (grad_spec_ref[pl.ds(row, 8), col(b)], grad_spec_ref[pl.ds(row + LEN, 8), col(b)]) for b in range(GROUP)
        ]
        for d in range(REACH):
            total_real, total_imag = 0.0, 0.0
            for block in range(GROUP):
                window = pairs[REACH + block - d]
                total_real += grads[block][0] * window[0] + grads[block][1] * window[1]
                total_imag += grads[block][1] * window[0] - grads[block][0] * window[1]
            product_ref[pl.ds(row, 8), col(d)] = total_real
            product_ref[pl.ds(row + LEN, 8), col(d)] = total_imag

    over_frequencies(step)
    terms = invert((inverse_high, inverse_low), product_ref[...])
    for d in range(REACH):
        terms_ref[d] = terms[:, col(d)].astype(BF16)
    copy.wait()


def correlate_back(place_ref, *refs):
    tables_hbm, (grad_spec_hbm, lag_spec_hbm, rounded_hbm, after_ref) = refs[:4], refs[4:8]
    out_refs, tables = refs[8 : 8 + GROUP], refs[8 + GROUP : 12 + GROUP]
    result_ref, after_spec_ref, product_ref, grad_spec_ref, lag_spec_ref, sems = refs[12 + GROUP :]
    place = place_ref[0]
    table_loads = [copy_out(tables_hbm[i], tables[i], sems.at[i]) for i in range(2)]
    loads = [
        copy_out(grad_spec_hbm, grad_spec_ref, sems.at[4]),
        copy_out(lag_spec_hbm, lag_spec_ref, sems.at[5]),
    ]
    table_loads += [copy_out(tables_hbm[i], tables[i], sems.at[i]) for i in range(2, 4)]
    copies = [
        copy_out(
            rounded_hbm.at[:, lane((place + step_number) & (GROUP - 1))],
            out_refs[step_number].at[LEN:, :],
            sems.at[6 + step_number],
        )
        for step_number in range(GROUP)
    ]
    (forward_high, forward_low), (inverse_high, inverse_low) = tables[:2], tables[2:]
    table_loads[0].wait()
    table_loads[1].wait()
    after_spec_ref[...] = spectrum((forward_high, forward_low), after_ref[...])
    for load in loads:
        load.wait()

    def step(row, sign):
        real = [grad_spec_ref[pl.ds(row, 8), col(b)] for b in range(GROUP)]
        real += [after_spec_ref[pl.ds(row, 8), col(b)] for b in range(REACH)]
        imag = [grad_spec_ref[pl.ds(row + LEN, 8), col(b)] for b in range(GROUP)]
        imag += [after_spec_ref[pl.ds(row + LEN, 8), col(b)] for b in range(REACH)]
        pairs = [
            (real[b] + sign * imag[b + 1], imag[b] - sign * real[b + 1]) for b in range(GROUP + REACH - 1)
        ]
        lag = [
            (lag_spec_ref[pl.ds(row, 8), col(d)], lag_spec_ref[pl.ds(row + LEN, 8), col(d)]) for d in range(REACH)
        ]
        for block in range(GROUP):
            total_real, total_imag = 0.0, 0.0
            for d in range(REACH):
                window = pairs[block + d]
                total_real += lag[d][0] * window[0] + lag[d][1] * window[1]
                total_imag += lag[d][0] * window[1] - lag[d][1] * window[0]
            product_ref[pl.ds(row, 8), col(block)] = total_real
            product_ref[pl.ds(row + LEN, 8), col(block)] = total_imag

    over_frequencies(step)
    table_loads[2].wait()
    table_loads[3].wait()
    result_ref[...] = invert((inverse_high, inverse_low), product_ref[...]).astype(BF16)
    for step_number in range(GROUP):
        out_refs[step_number][:LEN, :] = result_ref[:, lane((place + step_number) & (GROUP - 1))]
    for copy in copies:
        copy.wait()


def sum_terms(terms_ref, out_ref):
    groups = terms_ref.shape[0] // GROUP
    for place in range(GROUP):
        out_ref[:, col(place)] = sum(terms_ref[group * GROUP + place].astype(F32) for group in range(groups))


def finish(
    channels, place_ref, sums_ref, query_ref, key_ref, value_ref, cotangent_ref, factor_ref, *refs
):
    pieces = refs[:GROUP]
    normed_ref, grad_query_ref, grad_key_ref, grad_value_ref, lines_ref = refs[GROUP:]
    place = place_ref[0]
    half = GROUP // 2
    lines_ref[...] = row_lines(channels, sums_ref)
    lines = lines_ref[pl.ds(pl.multiple_of((place & 1) * LEN, LEN), LEN), :]
    number = lax.broadcasted_iota(jnp.int32, (LEN, GROUP), 1)
    inv = jnp.sum(jnp.where(number == place >> 1, lines, 0.0), axis=1, keepdims=True)
    mean = jnp.sum(jnp.where(number == half + (place >> 1), lines, 0.0), axis=1, keepdims=True)
    for step in range(GROUP):
        there = lane((place - step) & (GROUP - 1))
        piece = pieces[step]
        grad_mixed = piece[:LEN, :].astype(F32)
        grad_key_ref[:, there] = (grad_mixed * value_ref[:, there].astype(F32)).astype(BF16)
        grad_value_ref[:, there] = (grad_mixed * key_ref[:, there].astype(F32)).astype(BF16)
        factor = factor_ref[:, there]
        conv = piece[LEN:, :].astype(F32)
        normed = query_ref[:, there].astype(F32) * factor * conv * inv
        normed_ref[:, there] = normed.astype(BF16)
        grad_scaled = inv * (cotangent_ref[:, there].astype(F32) - normed * mean)
        grad_query_ref[:, there] = (grad_scaled * conv * factor).astype(BF16)


def on_chip(shape, dtype):
    return pltpu.VMEM(shape, dtype)


def off_chip(shape, dtype):
    return pltpu.HBM(shape, dtype)


def near(value):
    return pltpu.with_memory_space_constraint(value, pltpu.VMEM)


def far(value):
    return pltpu.with_memory_space_constraint(value, pltpu.HBM)


def call(body, outs, *args, scalars=0, scratch=(), copies=0, left=(), manual=(), cost=1000):
    specs = [pl.BlockSpec(memory_space=pltpu.SMEM)] * scalars
    specs += [
        pl.BlockSpec(memory_space=pl.ANY if index in left else pltpu.VMEM) for index in range(scalars, len(args))
    ]
    moved = sum(a.size * a.dtype.itemsize for a in args)
    return pl.pallas_call(
        body,
        out_shape=list(outs),
        in_specs=specs,
        out_specs=[pl.BlockSpec(memory_space=pl.ANY if i in manual else pltpu.VMEM) for i in range(len(outs))],
        scratch_shapes=[pltpu.VMEM(shape, dtype) for shape, dtype in scratch]
        + ([pltpu.SemaphoreType.DMA(copies)] if copies else []),
        cost_estimate=pl.CostEstimate(flops=cost, bytes_accessed=moved, transcendentals=0),
        compiler_params=pltpu.CompilerParams(vmem_limit_bytes=20 << 20),
    )(*args)


def swap(pieces):
    return [pieces[0]] + [
        lax.ppermute(pieces[step], "j", [(i, (i + step) % GROUP) for i in range(GROUP)]) for step in range(1, GROUP)
    ]


def trade(value, mask, groups):
    return lax.ppermute(value, "g", [(i, i ^ mask) for i in range(groups)])


def shards(query_proj, key_proj, value_proj, filters, cotangent, stock_id, stock_class, cond_table):
    groups = lax.axis_size("g")
    parts = lax.axis_size("ch")
    near_groups = min(4, groups)
    far_groups = groups // near_groups
    lag_rows = filters.shape[0]
    wide = GROUP * LANES
    half = wide // 2
    place = jnp.stack([lax.axis_index("j"), lax.axis_index("g")]).astype(jnp.int32)
    tables = [jnp.asarray(t) for t in transform_tables()]
    far_tables = list(map(far, tables))
    stock_id, stock_class = far(stock_id[None, :]), far(stock_class[None, :])
    table = far(jnp.pad(cond_table, ((0, 16 - cond_table.shape[0]), (0, 0))))

    (sent,) = call(
        pack, [off_chip((GROUP, ROWS, LANES), BF16)], *map(far, (key_proj, value_proj, query_proj, cotangent)),
        stock_id, stock_class, manual=(0,), copies=(2 * GROUP,),
        scratch=[((GROUP, CLASS, LANES), BF16), ((16, LANES), BF16)],
    )
    got = lax.all_to_all(sent, "j", 0, 0)
    lags = filters[None]
    lags = jnp.concatenate([lags] + [trade(lags, high * near_groups, groups) for high in range(1, far_groups)])
    lags = [lags] + [trade(lags, low, groups) for low in range(1, near_groups)]
    (lags,) = call(pack_lags, [off_chip((GROUP, groups * lag_rows, LANES), BF16)], *map(near, lags))
    got, lags = lax.optimization_barrier((got, lags))
    before = lax.ppermute(got[GROUP - REACH :, :LEN, :], "g", [(i, i + 1) for i in range(groups - 1)])
    got, lags = far(got), near(lax.all_to_all(lags, "j", 0, 0))
    own, gate, factor = call(
        prepare, [off_chip((2 * LEN, wide), F32), off_chip((LEN, wide), F32), off_chip((LEN, wide), F32)], place, table,
        got, stock_id, stock_class, *far_tables[:2], scalars=1, copies=(3,), manual=(0, 1, 2),
        scratch=[((2 * LEN, wide), F32), ((LEN, wide), F32), ((LEN, wide), F32)], cost=2 * 4 * LEN * LEN * wide,
    )
    results = call(
        functools.partial(convolve, near_groups, far_groups),
        [
            on_chip((2 * LEN, wide), F32), on_chip((LEN, wide), F32), on_chip((GROUP, LEN, LANES), BF16),
            on_chip((2 * LEN, half), F32), on_chip((LEN, wide), F32),
        ]
        + [on_chip(t.shape, BF16) for t in tables]
        + [off_chip((2 * LEN, half), F32), off_chip((LEN, wide), BF16), on_chip((GROUP * parts, 8, 2 * LEN), F32)],
        place, far(own), far(gate), got, before, lags, *far_tables, scalars=1, copies=(9,), manual=(9, 10),
        left=(1, 2, 3, 6, 7, 8, 9),
        scratch=[((2 * LEN, half), F32), ((LEN, wide), BF16), ((2 * LEN, wide), F32), ((LEN, half), F32)],
        cost=2 * 10 * LEN * LEN * wide,
    )
    own, gate, upstream, before_spec, conv, *near_tables = map(near, results[:9])
    lag_spec, rounded, sums = results[9:]
    sums = lax.all_to_all(sums, ("j", "ch"), 0, 0)
    grad_conv, first = call(
        functools.partial(finish_norm, wide * parts), [on_chip((LEN, wide), BF16), on_chip((LEN, half), BF16)],
        near(sums), conv, gate, upstream,
    )
    after = lax.ppermute(first, "g", [(i, i - 1) for i in range(1, groups)])
    grad_spec, terms = call(
        filter_terms, [off_chip((2 * LEN, wide), F32), off_chip((REACH, LEN, LANES), BF16)],
        near(grad_conv), own, before_spec, *near_tables, copies=(1,), manual=(0,),
        scratch=[((2 * LEN, half), F32), ((2 * LEN, wide), F32)],
        cost=2 * 7 * LEN * LEN * wide,
    )
    back = call(
        correlate_back, [on_chip((2 * LEN, LANES), BF16)] * GROUP, place, *far_tables, far(grad_spec), far(lag_spec),
        far(rounded), after, scalars=1, left=range(1, 8), copies=(6 + GROUP,),
        scratch=[(t.shape, BF16) for t in tables]
        + [
            ((LEN, wide), BF16), ((2 * LEN, half), F32), ((2 * LEN, wide), F32), ((2 * LEN, wide), F32),
            ((2 * LEN, half), F32),
        ],
        cost=2 * 8 * LEN * LEN * wide,
    )
    back = swap(back)
    terms = lax.all_to_all(terms.reshape(groups * GROUP, lag_rows, LANES), ("g", "j"), 0, 0)
    (grad_filter,) = call(sum_terms, [off_chip((lag_rows, wide), F32)], terms)
    outs = call(
        functools.partial(finish, wide * parts),
        [off_chip((LEN, wide), BF16)] * 4,
        place, far(sums), *map(near, (query_proj, key_proj, value_proj, cotangent, factor)), *map(near, back),
        scalars=1, scratch=[((2 * LEN, GROUP), F32)],
    )
    return *outs, grad_filter


def solution(mesh):
    ctx, ch = mesh.devices.shape
    inner = Mesh(mesh.devices.reshape(ctx // GROUP, GROUP, ch), ("g", "j", "ch"))
    rows = ("g", "j")
    return jax.shard_map(
        shards,
        mesh=inner,
        in_specs=(P(rows, "ch"),) * 5 + (P(rows), P(), P(None, "ch")),
        out_specs=(P(rows, "ch"),) * 5,
        check_vma=False,
    )
```

```python
import functools

import jax
import jax.numpy as jnp
import numpy as np
import ml_dtypes
from jax import lax
from jax.experimental import pallas as pl
from jax.experimental.pallas import tpu as pltpu
from jax.sharding import Mesh, PartitionSpec as P

GROUP = 8
REACH = 4
LEN = 256
LANES = 128
EPSILON = 1e-05
F32 = jnp.float32
BF16 = jnp.bfloat16


def split_table(table):
    high = table.astype(np.float32).astype(ml_dtypes.bfloat16)
    low = (table - high.astype(np.float64)).astype(ml_dtypes.bfloat16)
    return high, low


def transform_tables():
    number = np.concatenate([np.arange(0, LEN, 2), np.arange(1, LEN, 2)])
    angles = np.pi * ((2 * number[:, None] + 1) * np.arange(LEN)[None, :] % (4 * LEN)) / (2 * LEN)
    forward = np.concatenate([np.cos(angles), -np.sin(angles)], axis=0)
    return (*split_table(forward), *split_table(forward.T / LEN))


def dot(left, right):
    return jnp.dot(left, right, preferred_element_type=F32)


def halves(value):
    high = value.astype(BF16)
    return high, (value - high.astype(F32)).astype(BF16)


def lane(index):
    return pl.ds(pl.multiple_of(index * LANES, LANES), LANES)


def col(index):
    return slice(index * LANES, (index + 1) * LANES)


def event_classes(stock_ref, class_ref):
    stocks = class_ref.shape[1]
    hits = (lax.broadcasted_iota(jnp.int32, (stocks, LEN), 0) == stock_ref[...]).astype(F32).astype(BF16)
    classes = jnp.broadcast_to(class_ref[...].astype(F32), (8, stocks)).astype(BF16)
    return dot(classes, hits)


def modulation(event_class, table):
    high = table.astype(BF16)
    mid = (table - high.astype(F32)).astype(BF16)
    low = (table - high.astype(F32) - mid.astype(F32)).astype(BF16)
    number = lax.broadcasted_iota(jnp.int32, (table.shape[0], LEN), 0).astype(F32)
    hits = jnp.transpose((number == event_class).astype(F32)).astype(BF16)
    return 1.0 + (dot(hits, high) + dot(hits, mid) + dot(hits, low))


def copy_out(source, target, sem):
    copy = pltpu.make_async_copy(source, target, sem)
    copy.start()
    return copy


QUERY, UPSTREAM, CLASS, ROWS = LEN, 2 * LEN, 3 * LEN, 3 * LEN + 16


def pack(key_ref, value_ref, query_ref, cotangent_ref, stock_ref, class_ref, out_hbm, out_ref, sems):
    event_class = event_classes(stock_ref, class_ref).astype(BF16)
    copies = []
    for place in range(GROUP):
        product = key_ref[:, col(place)].astype(F32) * value_ref[:, col(place)].astype(F32)
        out_ref[place, :LEN, :] = product.astype(BF16)
        out_ref[place, QUERY:UPSTREAM, :] = query_ref[:, col(place)]
        out_ref[place, UPSTREAM:CLASS, :] = cotangent_ref[:, col(place)]
        out_ref[place, CLASS : CLASS + 8, :] = event_class[:, :LANES]
        out_ref[place, CLASS + 8 :, :] = event_class[:, LANES:]
        copies.append(copy_out(out_ref.at[place], out_hbm.at[place], sems.at[place]))
    for copy in copies:
        copy.wait()


def pack_lags(*refs):
    out_ref, first = refs[-1], 0
    for lags_ref in refs[:-1]:
        rows = lags_ref.shape[1]
        for high in range(lags_ref.shape[0]):
            for place in range(GROUP):
                out_ref[place, first : first + rows, :] = lags_ref[high, :, col(place)]
            first += rows


def spectrum(forward, rows):
    return dot(forward[0][...], rows) + dot(forward[1][...], rows)


def invert(inverse, spec):
    high, low = halves(spec)
    return dot(inverse[0][...], high) + (dot(inverse[0][...], low) + dot(inverse[1][...], high))


def over_frequencies(step):
    for half in range(2):
        @pl.loop(0, LEN // 16)
        def _(chunk):
            step(pl.multiple_of(half * (LEN // 2) + chunk * 8, 8), 1.0 - 2.0 * half)


def windows(real, imag, sign):
    pairs = {}
    for block in range(1, len(real)):
        pairs[block] = (real[block] - sign * imag[block - 1], imag[block] + sign * real[block - 1])
    return pairs


def read_blocks(own_ref, before_ref, row):
    real = [before_ref[pl.ds(row, 8), col(block)] for block in range(REACH)]
    real += [own_ref[pl.ds(row, 8), col(block)] for block in range(GROUP)]
    imag = [before_ref[pl.ds(row + LEN, 8), col(block)] for block in range(REACH)]
    imag += [own_ref[pl.ds(row + LEN, 8), col(block)] for block in range(GROUP)]
    return real, imag


def prepare(place_ref, table_ref, got_ref, forward_high, forward_low, own_out, gate_out, own_ref, gate_ref, sems):
    rows = jnp.concatenate([got_ref[b, :LEN, :] for b in range(GROUP)], axis=1)
    own_ref[...] = spectrum((forward_high, forward_low), rows)
    copies = [copy_out(own_ref, own_out, sems.at[0])]
    table = table_ref[:, lane(place_ref[0])]
    for block in range(GROUP):
        classes = got_ref[block, CLASS:, :].astype(F32)
        event_class = jnp.concatenate([classes[:1], classes[8:9]], axis=1)
        gate_ref[:, col(block)] = got_ref[block, QUERY:UPSTREAM, :].astype(F32) * modulation(event_class, table)
    copies.append(copy_out(gate_ref, gate_out, sems.at[1]))
    for copy in copies:
        copy.wait()


def convolve(near_groups, far_groups, place_ref, own_hbm, gate_hbm, got_hbm, before_ref, lags_ref, *refs):
    own_ref, gate_ref, upstream_ref, before_spec_ref, conv_ref = refs[4:9]
    forward, inverse = refs[9:11], refs[11:13]
    lag_spec_hbm, rounded_hbm, sums_ref, lag_spec_ref, rounded_ref, product_ref, sorted_ref, sems = refs[13:]
    tables = [copy_out(refs[i], refs[9 + i], sems.at[5 + i]) for i in range(4)]
    loads = [
        copy_out(own_hbm, own_ref, sems.at[0]),
        copy_out(gate_hbm, gate_ref, sems.at[1]),
        copy_out(got_hbm.at[:, UPSTREAM:CLASS, :], upstream_ref, sems.at[2]),
    ]
    group = place_ref[1]
    tables[0].wait()
    tables[1].wait()
    before_spec_ref[...] = spectrum(forward, jnp.concatenate([before_ref[b] for b in range(REACH)], axis=1))
    rows = lags_ref.shape[1] // (near_groups * far_groups)
    for low in range(near_groups):
        for high in range(far_groups):
            at = (low * far_groups + high) * rows
            first = (group ^ (high * near_groups + low)) * (GROUP * rows)
            row = pl.multiple_of(first & (LEN - 1), GROUP * rows)
            piece = lags_ref[:, at : at + rows, :].astype(F32).reshape(GROUP * rows, LANES)
            sorted_ref[pl.ds(row, GROUP * rows), lane(first // LEN)] = piece
    lag_spec_ref[...] = spectrum(forward, sorted_ref[...].astype(BF16))
    copies = [copy_out(lag_spec_ref, lag_spec_hbm, sems.at[4])]
    loads[0].wait()

    def step(row, sign):
        real, imag = read_blocks(own_ref, before_spec_ref, row)
        pairs = windows(real, imag, sign)
        lag = [
            (lag_spec_ref[pl.ds(row, 8), col(d)], lag_spec_ref[pl.ds(row + LEN, 8), col(d)]) for d in range(REACH)
        ]
        for block in range(GROUP):
            total_real, total_imag = 0.0, 0.0
            for d in range(REACH):
                window = pairs[REACH + block - d]
                total_real += lag[d][0] * window[0] - lag[d][1] * window[1]
                total_imag += lag[d][0] * window[1] + lag[d][1] * window[0]
            product_ref[pl.ds(row, 8), col(block)] = total_real
            product_ref[pl.ds(row + LEN, 8), col(block)] = total_imag

    over_frequencies(step)
    tables[2].wait()
    tables[3].wait()
    conv = invert(inverse, product_ref[...])
    conv_ref[...] = conv
    rounded_ref[...] = conv.astype(BF16)
    copies.append(copy_out(rounded_ref, rounded_hbm, sems.at[3]))
    loads[1].wait()
    loads[2].wait()
    ones = jnp.ones((8, LANES), BF16)

    def channel_sum(value):
        contract = (((1,), (1,)), ((), ()))
        return sum(lax.dot_general(ones, part, contract, preferred_element_type=F32) for part in halves(value))[:1]

    lines = [[], []]
    for block in range(GROUP):
        scaled = gate_ref[:, col(block)] * conv[:, col(block)]
        lines[0].append(channel_sum(scaled * scaled))
        lines[1].append(channel_sum(scaled * upstream_ref[block].astype(F32)))
    for index in range(2):
        for pair in range(GROUP // 2):
            both = jnp.concatenate(lines[index][2 * pair : 2 * pair + 2], axis=1)
            line = index * (GROUP // 2) + pair
            for peer in range(sums_ref.shape[0]):
                sums_ref[peer, line : line + 1, :] = both
    for copy in copies:
        copy.wait()


def row_lines(channels, sums_ref):
    total = jnp.sum(sums_ref[...], axis=0)
    half = GROUP // 2
    inv_rms = lax.rsqrt(total[:half] / channels + EPSILON)
    return jnp.transpose(jnp.concatenate([inv_rms, total[half:] * inv_rms / channels], axis=0))


def finish_norm(channels, sums_ref, conv_ref, gate_ref, upstream_ref, grad_ref, first_ref):
    lines = row_lines(channels, sums_ref)
    half = GROUP // 2
    for block in range(GROUP):
        rows = slice((block % 2) * LEN, (block % 2 + 1) * LEN)
        inv = lines[rows, block // 2 : block // 2 + 1]
        mean = lines[rows, half + block // 2 : half + block // 2 + 1]
        gate = gate_ref[:, col(block)]
        normed = gate * conv_ref[:, col(block)] * inv
        grad_conv = (inv * (upstream_ref[block].astype(F32) - normed * mean) * gate).astype(BF16)
        grad_ref[:, col(block)] = grad_conv
        if block < REACH:
            first_ref[:, col(block)] = grad_conv


def filter_terms(
    grad_ref, own_ref, before_ref, forward_high, forward_low, inverse_high, inverse_low, grad_hbm, terms_ref,
    product_ref, grad_spec_ref, sems,
):
    grad_spec_ref[...] = spectrum((forward_high, forward_low), grad_ref[...])
    copy = copy_out(grad_ref, grad_hbm, sems.at[0])

    def step(row, sign):
        real, imag = read_blocks(own_ref, before_ref, row)
        pairs = windows(real, imag, sign)
        grads = [
            (grad_spec_ref[pl.ds(row, 8), col(b)], grad_spec_ref[pl.ds(row + LEN, 8), col(b)]) for b in range(GROUP)
        ]
        for d in range(REACH):
            total_real, total_imag = 0.0, 0.0
            for block in range(GROUP):
                window = pairs[REACH + block - d]
                total_real += grads[block][0] * window[0] + grads[block][1] * window[1]
                total_imag += grads[block][1] * window[0] - grads[block][0] * window[1]
            product_ref[pl.ds(row, 8), col(d)] = total_real
            product_ref[pl.ds(row + LEN, 8), col(d)] = total_imag

    over_frequencies(step)
    terms = invert((inverse_high, inverse_low), product_ref[...])
    for d in range(REACH):
        terms_ref[d] = terms[:, col(d)].astype(BF16)
    copy.wait()


def correlate_back(place_ref, *refs):
    tables_hbm, (grad_hbm, lag_spec_hbm, rounded_hbm, after_ref) = refs[:4], refs[4:8]
    out_refs, tables = refs[8 : 8 + GROUP], refs[8 + GROUP : 12 + GROUP]
    result_ref, after_spec_ref, product_ref, grad_spec_ref, lag_spec_ref, grad_ref, sems = refs[12 + GROUP :]
    place = place_ref[0]
    table_loads = [copy_out(tables_hbm[i], tables[i], sems.at[i]) for i in range(2)]
    loads = [
        copy_out(grad_hbm, grad_ref, sems.at[4]),
        copy_out(lag_spec_hbm, lag_spec_ref, sems.at[5]),
    ]
    table_loads += [copy_out(tables_hbm[i], tables[i], sems.at[i]) for i in range(2, 4)]
    copies = [
        copy_out(
            rounded_hbm.at[:, lane((place + step_number) & (GROUP - 1))],
            out_refs[step_number].at[LEN:, :],
            sems.at[6 + step_number],
        )
        for step_number in range(GROUP)
    ]
    (forward_high, forward_low), (inverse_high, inverse_low) = tables[:2], tables[2:]
    table_loads[0].wait()
    table_loads[1].wait()
    after_spec_ref[...] = spectrum((forward_high, forward_low), after_ref[...])
    loads[0].wait()
    grad_spec_ref[...] = spectrum((forward_high, forward_low), grad_ref[...])
    loads[1].wait()

    def step(row, sign):
        real = [grad_spec_ref[pl.ds(row, 8), col(b)] for b in range(GROUP)]
        real += [after_spec_ref[pl.ds(row, 8), col(b)] for b in range(REACH)]
        imag = [grad_spec_ref[pl.ds(row + LEN, 8), col(b)] for b in range(GROUP)]
        imag += [after_spec_ref[pl.ds(row + LEN, 8), col(b)] for b in range(REACH)]
        pairs = [
            (real[b] + sign * imag[b + 1], imag[b] - sign * real[b + 1]) for b in range(GROUP + REACH - 1)
        ]
        lag = [
            (lag_spec_ref[pl.ds(row, 8), col(d)], lag_spec_ref[pl.ds(row + LEN, 8), col(d)]) for d in range(REACH)
        ]
        for block in range(GROUP):
            total_real, total_imag = 0.0, 0.0
            for d in range(REACH):
                window = pairs[block + d]
                total_real += lag[d][0] * window[0] + lag[d][1] * window[1]
                total_imag += lag[d][0] * window[1] - lag[d][1] * window[0]
            product_ref[pl.ds(row, 8), col(block)] = total_real
            product_ref[pl.ds(row + LEN, 8), col(block)] = total_imag

    over_frequencies(step)
    table_loads[2].wait()
    table_loads[3].wait()
    result_ref[...] = invert((inverse_high, inverse_low), product_ref[...]).astype(BF16)
    for step_number in range(GROUP):
        out_refs[step_number][:LEN, :] = result_ref[:, lane((place + step_number) & (GROUP - 1))]
    for copy in copies:
        copy.wait()


def sum_terms(terms_ref, out_ref):
    groups = terms_ref.shape[0] // GROUP
    for place in range(GROUP):
        out_ref[:, col(place)] = sum(terms_ref[group * GROUP + place].astype(F32) for group in range(groups))


def finish(
    channels, place_ref, sums_ref, query_ref, key_ref, value_ref, cotangent_ref, stock_ref, class_ref, table_ref, *refs
):
    pieces = refs[:GROUP]
    normed_ref, grad_query_ref, grad_key_ref, grad_value_ref, factor_ref, lines_ref = refs[GROUP:]
    place = place_ref[0]
    half = GROUP // 2
    lines_ref[...] = row_lines(channels, sums_ref)
    lines = lines_ref[pl.ds(pl.multiple_of((place & 1) * LEN, LEN), LEN), :]
    number = lax.broadcasted_iota(jnp.int32, (LEN, GROUP), 1)
    inv = jnp.sum(jnp.where(number == place >> 1, lines, 0.0), axis=1, keepdims=True)
    mean = jnp.sum(jnp.where(number == half + (place >> 1), lines, 0.0), axis=1, keepdims=True)
    factor_ref[...] = modulation(event_classes(stock_ref, class_ref)[:1], table_ref[...])
    for step in range(GROUP):
        there = lane((place - step) & (GROUP - 1))
        piece = pieces[step]
        grad_mixed = piece[:LEN, :].astype(F32)
        grad_key_ref[:, there] = (grad_mixed * value_ref[:, there].astype(F32)).astype(BF16)
        grad_value_ref[:, there] = (grad_mixed * key_ref[:, there].astype(F32)).astype(BF16)
        factor = factor_ref[:, there]
        conv = piece[LEN:, :].astype(F32)
        normed = query_ref[:, there].astype(F32) * factor * conv * inv
        normed_ref[:, there] = normed.astype(BF16)
        grad_scaled = inv * (cotangent_ref[:, there].astype(F32) - normed * mean)
        grad_query_ref[:, there] = (grad_scaled * conv * factor).astype(BF16)


def on_chip(shape, dtype):
    return pltpu.VMEM(shape, dtype)


def off_chip(shape, dtype):
    return pltpu.HBM(shape, dtype)


def near(value):
    return pltpu.with_memory_space_constraint(value, pltpu.VMEM)


def far(value):
    return pltpu.with_memory_space_constraint(value, pltpu.HBM)


def call(body, outs, *args, scalars=0, scratch=(), copies=0, left=(), manual=(), cost=1000):
    specs = [pl.BlockSpec(memory_space=pltpu.SMEM)] * scalars
    specs += [
        pl.BlockSpec(memory_space=pl.ANY if index in left else pltpu.VMEM) for index in range(scalars, len(args))
    ]
    moved = sum(a.size * a.dtype.itemsize for a in args)
    return pl.pallas_call(
        body,
        out_shape=list(outs),
        in_specs=specs,
        out_specs=[pl.BlockSpec(memory_space=pl.ANY if i in manual else pltpu.VMEM) for i in range(len(outs))],
        scratch_shapes=[pltpu.VMEM(shape, dtype) for shape, dtype in scratch]
        + ([pltpu.SemaphoreType.DMA(copies)] if copies else []),
        cost_estimate=pl.CostEstimate(flops=cost, bytes_accessed=moved, transcendentals=0),
        compiler_params=pltpu.CompilerParams(vmem_limit_bytes=20 << 20),
    )(*args)


def swap(pieces):
    return [pieces[0]] + [
        lax.ppermute(pieces[step], "j", [(i, (i + step) % GROUP) for i in range(GROUP)]) for step in range(1, GROUP)
    ]


def trade(value, mask, groups):
    return lax.ppermute(value, "g", [(i, i ^ mask) for i in range(groups)])


def shards(query_proj, key_proj, value_proj, filters, cotangent, stock_id, stock_class, cond_table):
    groups = lax.axis_size("g")
    parts = lax.axis_size("ch")
    near_groups = min(4, groups)
    far_groups = groups // near_groups
    lag_rows = filters.shape[0]
    wide = GROUP * LANES
    half = wide // 2
    place = jnp.stack([lax.axis_index("j"), lax.axis_index("g")]).astype(jnp.int32)
    tables = [jnp.asarray(t) for t in transform_tables()]
    far_tables = list(map(far, tables))
    stock_id, stock_class = far(stock_id[None, :]), far(stock_class[None, :])
    table = far(jnp.pad(cond_table, ((0, 16 - cond_table.shape[0]), (0, 0))))

    (sent,) = call(
        pack, [off_chip((GROUP, ROWS, LANES), BF16)], *map(far, (key_proj, value_proj, query_proj, cotangent)),
        stock_id, stock_class, manual=(0,), copies=(GROUP,), scratch=[((GROUP, ROWS, LANES), BF16)],
    )
    got = lax.all_to_all(sent, "j", 0, 0)
    lags = filters[None]
    lags = jnp.concatenate([lags] + [trade(lags, high * near_groups, groups) for high in range(1, far_groups)])
    lags = [lags] + [trade(lags, low, groups) for low in range(1, near_groups)]
    (lags,) = call(pack_lags, [off_chip((GROUP, groups * lag_rows, LANES), BF16)], *map(near, lags))
    got, lags = lax.optimization_barrier((got, lags))
    before = lax.ppermute(got[GROUP - REACH :, :LEN, :], "g", [(i, i + 1) for i in range(groups - 1)])
    got, lags = far(got), near(lax.all_to_all(lags, "j", 0, 0))
    own, gate = call(
        prepare, [off_chip((2 * LEN, wide), F32), off_chip((LEN, wide), F32)], place, table, got, *far_tables[:2],
        scalars=1, copies=(2,), manual=(0, 1), scratch=[((2 * LEN, wide), F32), ((LEN, wide), F32)],
        cost=2 * 4 * LEN * LEN * wide,
    )
    results = call(
        functools.partial(convolve, near_groups, far_groups),
        [
            on_chip((2 * LEN, wide), F32), on_chip((LEN, wide), F32), on_chip((GROUP, LEN, LANES), BF16),
            on_chip((2 * LEN, half), F32), on_chip((LEN, wide), F32),
        ]
        + [on_chip(t.shape, BF16) for t in tables]
        + [off_chip((2 * LEN, half), F32), off_chip((LEN, wide), BF16), on_chip((GROUP * parts, 8, 2 * LEN), F32)],
        place, far(own), far(gate), got, before, lags, *far_tables, scalars=1, copies=(9,), manual=(9, 10),
        left=(1, 2, 3, 6, 7, 8, 9),
        scratch=[((2 * LEN, half), F32), ((LEN, wide), BF16), ((2 * LEN, wide), F32), ((LEN, half), F32)],
        cost=2 * 10 * LEN * LEN * wide,
    )
    own, gate, upstream, before_spec, conv, *near_tables = map(near, results[:9])
    lag_spec, rounded, sums = results[9:]
    sums = lax.all_to_all(sums, ("j", "ch"), 0, 0)
    grad_conv, first = call(
        functools.partial(finish_norm, wide * parts), [on_chip((LEN, wide), BF16), on_chip((LEN, half), BF16)],
        near(sums), conv, gate, upstream,
    )
    after = lax.ppermute(first, "g", [(i, i - 1) for i in range(1, groups)])
    grad_spec, terms = call(
        filter_terms, [off_chip((LEN, wide), BF16), off_chip((REACH, LEN, LANES), BF16)],
        near(grad_conv), own, before_spec, *near_tables, copies=(1,), manual=(0,),
        scratch=[((2 * LEN, half), F32), ((2 * LEN, wide), F32)],
        cost=2 * 7 * LEN * LEN * wide,
    )
    back = call(
        correlate_back, [on_chip((2 * LEN, LANES), BF16)] * GROUP, place, *far_tables, far(grad_spec), far(lag_spec),
        far(rounded), after, scalars=1, left=range(1, 8), copies=(6 + GROUP,),
        scratch=[(t.shape, BF16) for t in tables]
        + [
            ((LEN, wide), BF16), ((2 * LEN, half), F32), ((2 * LEN, wide), F32), ((2 * LEN, wide), F32),
            ((2 * LEN, half), F32), ((LEN, wide), BF16),
        ],
        cost=2 * 8 * LEN * LEN * wide,
    )
    back = swap(back)
    terms = lax.all_to_all(terms.reshape(groups * GROUP, lag_rows, LANES), ("g", "j"), 0, 0)
    (grad_filter,) = call(sum_terms, [off_chip((lag_rows, wide), F32)], terms)
    outs = call(
        functools.partial(finish, wide * parts),
        [off_chip((LEN, wide), BF16)] * 4,
        place, far(sums), *map(near, (query_proj, key_proj, value_proj, cotangent)), stock_id, stock_class, table,
        *map(near, back), scalars=1, scratch=[((LEN, wide), F32), ((2 * LEN, GROUP), F32)],
    )
    return *outs, grad_filter


def solution(mesh):
    ctx, ch = mesh.devices.shape
    inner = Mesh(mesh.devices.reshape(ctx // GROUP, GROUP, ch), ("g", "j", "ch"))
    rows = ("g", "j")
    return jax.shard_map(
        shards,
        mesh=inner,
        in_specs=(P(rows, "ch"),) * 5 + (P(rows), P(), P(None, "ch")),
        out_specs=(P(rows, "ch"),) * 5,
        check_vma=False,
    )
```
